256 devices in a mesh: req: 32 (over y, x, core), tp: 8 (over z).
Axes of the slice: x: 4, y: 4, z: 8, core: 2. Of those that a mesh axis runs over, the one named last changes fastest.
Arguments:
- tokens: bfloat16 [32, 768, 2048], P('req', None, 'tp'), may hold values from -6 to 6
- q_weight: bfloat16 [2048, 2048], P(None, 'tp'), may hold values from -0.125 to 0.125
- k_weight: bfloat16 [2048, 2048], P(None, 'tp'), may hold values from -0.125 to 0.125
- v_weight: bfloat16 [2048, 2048], P(None, 'tp'), may hold values from -0.125 to 0.125
- o_weight: bfloat16 [2048, 2048], P('tp'), may hold values from -0.125 to 0.125
- q_gain: bfloat16 [2048], P('tp'), may hold values from 0.099609375 to 1.8984375
- k_gain: bfloat16 [2048], P('tp'), may hold values from 0.099609375 to 1.8984375
- post_gain: bfloat16 [2048], P('tp'), may hold values from 0.099609375 to 1.8984375
- key_pool: bfloat16 [1024, 128, 2048], P('req', None, 'tp'), may hold values from -400 to 400
- value_pool: bfloat16 [1024, 128, 2048], P('req', None, 'tp'), may hold values from -6 to 6
- cache_len: int32 [32], replicated, may hold values from 1 to 4096, as said below
- page_table: int32 [32, 32], replicated, may hold values from -1 to 1023, as said below
Outputs:
- mixed: bfloat16 [32, 768, 2048], P('req', None, 'tp')
- new_keys: bfloat16 [32, 768, 2048], P('req', None, 'tp')
- new_values: bfloat16 [32, 768, 2048], P('req', None, 'tp')
The draws below stay inside these ranges and needn't reach their ends.
Inputs may be any that keep to these rules, and one draw needn't show every extreme that they name: `cache_len`: on some index of req the one request hold 4096 cached tokens. `page_table`: entry p of request r is a pool page (index d * 32 + local page of index d of req) for p < ceil(cache_len[r] / 128) and -1 otherwise; no pool page is named twice; the pages named by the requests of one index of req lie at most 1 on any one index of req, and some pair of indices reaches 1.
All inputs are finite; a program needn't handle non-finite values.
Results may differ from the reference program's by a relative error of at most 0.013.
Values may be sent and summed in bfloat16 or wider, within the bound.
No kernel may reach another device: no remote copies, remote signals or barrier semaphores. Data moves between devices by JAX's collectives and lax.ppermute only.
A program may use at most 64 MiB of HBM per device.

```python
import jax
import jax.numpy as jnp
from jax import lax

D = 2048
HEADS = 16
HEAD_DIM = 128
BLOCK = 768
REQ_DEV = 1
PAGE = 128
MAXLEN = 4096
MAXPAGES = 32
REQS = 32
POOLS = 1024
N_TP = 8


def request_lengths(key):
    owners = REQS // REQ_DEV
    lengths = jax.random.randint(jax.random.fold_in(key, 11), (REQS,), 1, MAXLEN + 1)
    chosen = jax.random.randint(jax.random.fold_in(key, 14), (), 0, owners)
    owner_of = jnp.arange(REQS) // REQ_DEV
    return jnp.where(owner_of == chosen, MAXLEN, lengths).astype(jnp.int32)


def draw_cache_len(key, part):
    return request_lengths(key)


def draw_page_table(key, part):
    lengths = request_lengths(key)
    owners = REQS // REQ_DEV
    per_owner = REQ_DEV * MAXPAGES
    pool_dev = per_owner
    pair_cap = pool_dev // owners
    page_count = (lengths + PAGE - 1) // PAGE
    valid = (jnp.arange(MAXPAGES)[None, :] < page_count[:, None]).reshape(owners, per_owner)
    offsets = jax.random.randint(jax.random.fold_in(key, 12), (owners, 1), 0, owners)
    source = (offsets + jnp.arange(per_owner)[None, :]) % owners
    order = jnp.arange(per_owner)
    same = (source[:, :, None] == source[:, None, :]) & valid[:, None, :] & (order[None, :, None] > order[None, None, :])
    rank = jnp.sum(same.astype(jnp.int32), -1)
    shuffles = jax.vmap(lambda sub_key: jax.random.permutation(sub_key, pool_dev))(jax.random.split(jax.random.fold_in(key, 13), owners))
    owner_ids = jnp.arange(owners)[:, None]
    slot_ids = jnp.clip(owner_ids * pair_cap + rank, 0, pool_dev - 1)
    local = shuffles[source, slot_ids]
    table = jnp.where(valid, source * pool_dev + local, -1)
    return table.reshape(REQS, MAXPAGES).astype(jnp.int32)


def draw_key_pool(key, part):
    base = jax.random.normal(jax.random.fold_in(key, 21), (POOLS, PAGE, HEADS * HEAD_DIM), jnp.float32)
    base = jnp.clip(base, -6.0, 6.0)
    return base.astype(jnp.bfloat16)


def levels(stream_key, extent, pieces, least, high):
    def one(axis_at, parts):
        steps = jax.random.uniform(jax.random.fold_in(jax.random.fold_in(stream_key, 6), axis_at), (parts,), jnp.float32, least / len(pieces), high / len(pieces))
        return jnp.repeat(jnp.exp(steps), extent[axis_at] // parts).reshape((-1,) + (1,) * (len(extent) - axis_at - 1))

    level = one(*pieces[0])
    for cut in pieces[1:]:
        level = level * one(*cut)
    return level


def noise(rng, extent, scale, reach, cuts=(), held_as=jnp.bfloat16):
    entries = jax.random.normal(rng, extent, jnp.float32) * scale
    if len(cuts) > 0:
        entries = levels(rng, extent, cuts, -0.22, 0.18) * entries
    return jnp.clip(entries, min=-reach, max=reach).astype(held_as)


def setup_inputs(seed: int = 0) -> dict:
    key_list = jax.random.split(jax.random.key(seed), 13)
    tokens = noise(key_list[0], (REQS, BLOCK, D), 1.0, 6.0, ((0, 32), (2, 8)))
    q_weight = noise(key_list[1], (D, HEADS * HEAD_DIM), D ** -0.5, 0.125, ((1, 8),))
    k_weight = noise(key_list[2], (D, HEADS * HEAD_DIM), D ** -0.5, 0.125, ((1, 8),))
    v_weight = noise(key_list[3], (D, HEADS * HEAD_DIM), D ** -0.5, 0.125, ((1, 8),))
    o_weight = noise(key_list[4], (HEADS * HEAD_DIM, D), (HEADS * HEAD_DIM) ** -0.5, 0.125, ((0, 8),))
    q_gain = jnp.clip(1.0 + 0.18 * jax.random.normal(key_list[5], (HEADS * HEAD_DIM,), jnp.float32), 0.099609375, 1.8984375).astype(jnp.bfloat16)
    k_gain = jnp.clip(1.0 + 0.18 * jax.random.normal(key_list[6], (HEADS * HEAD_DIM,), jnp.float32), 0.099609375, 1.8984375).astype(jnp.bfloat16)
    post_gain = jnp.clip(1.0 + 0.18 * jax.random.normal(key_list[7], (D,), jnp.float32), 0.099609375, 1.8984375).astype(jnp.bfloat16)
    key_pool = draw_key_pool(jax.random.fold_in(key_list[12], 71), 0)
    value_pool = noise(key_list[9], (POOLS, PAGE, HEADS * HEAD_DIM), 1.0, 6.0, ((0, 32), (2, 8)))
    cache_len = draw_cache_len(jax.random.fold_in(key_list[12], 71), 0)
    page_table = draw_page_table(jax.random.fold_in(key_list[12], 71), 0)
    return {"tokens": tokens, "q_weight": q_weight, "k_weight": k_weight, "v_weight": v_weight, "o_weight": o_weight, "q_gain": q_gain, "k_gain": k_gain, "post_gain": post_gain, "key_pool": key_pool, "value_pool": value_pool, "cache_len": cache_len, "page_table": page_table}


EPSILON = 1e-06
ROPE_BASE = 500000.0

def rotate(values, positions):
    half_dim = values.shape[-1] // 2
    freqs = jnp.power(jnp.float32(ROPE_BASE), -jnp.arange(half_dim, dtype=jnp.float32) * 2.0 / values.shape[-1])
    angles = positions[..., None] * freqs
    cosine = jnp.cos(angles)[..., None, :]
    sine_part = jnp.sin(angles)[..., None, :]
    first_half = values[..., :half_dim]
    second_half = values[..., half_dim:]
    return jnp.concatenate([first_half * cosine - second_half * sine_part, second_half * cosine + first_half * sine_part], -1)

def attend(query, cache_k, cache_v, fresh_k, fresh_v, lengths):
    scale = query.shape[-1] ** (-0.5)
    block_len = query.shape[1]
    cache_span = cache_k.shape[1]
    query_f = query.astype(jnp.float32)
    cache_scores = jnp.einsum('rqhd,rkhd->rhqk', query_f, cache_k.astype(jnp.float32)) * scale
    fresh_scores = jnp.einsum('rqhd,rkhd->rhqk', query_f, fresh_k.astype(jnp.float32)) * scale
    cache_mask = (jnp.arange(cache_span)[None, :] < lengths[:, None])[:, None, None, :]
    causal = (jnp.arange(block_len)[:, None] >= jnp.arange(block_len)[None, :])[None, None]
    scores = jnp.concatenate([jnp.where(cache_mask, cache_scores, -1e+30), jnp.where(causal, fresh_scores, -1e+30)], -1)
    peak = lax.optimization_barrier(jnp.max(scores, -1, keepdims=True))
    raised = jnp.exp(scores - peak)
    weights = (raised / lax.optimization_barrier(jnp.sum(raised, -1, keepdims=True))).astype(jnp.bfloat16)
    weights_f = weights.astype(jnp.float32)
    result = jnp.einsum('rhqk,rkhd->rqhd', weights_f[..., :cache_span], cache_v.astype(jnp.float32))
    result = result + jnp.einsum('rhqk,rkhd->rqhd', weights_f[..., cache_span:], fresh_v.astype(jnp.float32))
    return result.astype(jnp.bfloat16).reshape(query.shape[0], block_len, -1)

def reference(tokens, q_weight, k_weight, v_weight, o_weight, q_gain, k_gain, post_gain, key_pool, value_pool, cache_len, page_table):
    row_count = REQS * BLOCK
    columns = HEADS * HEAD_DIM
    flat = tokens.reshape(row_count, D)
    q_proj = jnp.dot(flat, q_weight, preferred_element_type=jnp.float32)
    k_proj = jnp.dot(flat, k_weight, preferred_element_type=jnp.float32)
    new_values = jnp.dot(flat, v_weight, preferred_element_type=jnp.float32).astype(jnp.bfloat16)
    q_normed = q_proj * lax.rsqrt(lax.optimization_barrier(jnp.mean(q_proj * q_proj, 1)) + EPSILON)[:, None] * q_gain.astype(jnp.float32)
    k_normed = k_proj * lax.rsqrt(lax.optimization_barrier(jnp.mean(k_proj * k_proj, 1)) + EPSILON)[:, None] * k_gain.astype(jnp.float32)
    positions = (cache_len[:, None] + jnp.arange(BLOCK, dtype=jnp.int32)[None, :]).astype(jnp.float32)
    query = rotate(q_normed.reshape(REQS, BLOCK, HEADS, HEAD_DIM), positions).astype(jnp.bfloat16)
    new_keys = rotate(k_normed.reshape(REQS, BLOCK, HEADS, HEAD_DIM), positions).astype(jnp.bfloat16)
    fresh_values = new_values.reshape(REQS, BLOCK, HEADS, HEAD_DIM)

    def one_request(items):
        query_r, key_r, value_r, length_r, table_r = items
        chosen = jnp.maximum(table_r, 0).astype(jnp.int32)
        cache_k = key_pool[chosen].reshape(MAXLEN, HEADS, HEAD_DIM)
        cache_v = value_pool[chosen].reshape(MAXLEN, HEADS, HEAD_DIM)
        return attend(query_r[None], cache_k[None], cache_v[None], key_r[None], value_r[None], length_r[None])[0]
    attended = lax.map(one_request, (query, new_keys, fresh_values, cache_len, page_table))
    attended = attended.reshape(row_count, columns)
    group = columns // N_TP
    projected = jnp.zeros((row_count, D), jnp.float32)
    for index in range(N_TP):
        part = jnp.dot(attended[:, index * group:(index + 1) * group], o_weight[index * group:(index + 1) * group], preferred_element_type=jnp.float32)
        rounded = lax.optimization_barrier(part.astype(jnp.bfloat16))
        projected = projected + rounded.astype(jnp.float32)
    normed = projected * lax.rsqrt(lax.optimization_barrier(jnp.mean(projected * projected, 1)) + EPSILON)[:, None]
    mixed = (flat.astype(jnp.float32) + normed * post_gain.astype(jnp.float32)).astype(jnp.bfloat16)
    return (mixed.reshape(REQS, BLOCK, D), new_keys.reshape(REQS, BLOCK, columns), new_values.reshape(REQS, BLOCK, columns))
```

```python
import functools

import jax
import jax.numpy as jnp
from jax import lax
from jax.experimental import pallas as pl
from jax.experimental.pallas import tpu as pltpu
from jax.sharding import PartitionSpec as P

HEAD_DIM = 128
EPSILON = 1e-06
ROPE_BASE = 500000.0
NEG = -1e30
F32 = jnp.float32
BF16 = jnp.bfloat16
VMEM_SPEC = pl.BlockSpec(memory_space=pltpu.VMEM)
SMEM_SPEC = pl.BlockSpec(memory_space=pltpu.SMEM)
ANY_SPEC = pl.BlockSpec(memory_space=pl.ANY)


def cost(flops, moved):
    return pl.CostEstimate(flops=flops, bytes_accessed=moved, transcendentals=0)


def params(mib):
    return pltpu.CompilerParams(vmem_limit_bytes=mib << 20)


def pick_kernel(chosen, key_pool, value_pool, out, sem):
    slots = out.shape[0]
    page = key_pool.shape[1]

    def copies(slot):
        index = chosen[slot]
        return (
            pltpu.make_async_copy(key_pool.at[index], out.at[slot, pl.ds(0, page)], sem.at[0, slot]),
            pltpu.make_async_copy(
                value_pool.at[index], out.at[slot, pl.ds(page, page)], sem.at[1, slot]
            ),
        )

    @pl.loop(0, slots)
    def _(slot):
        for copy in copies(slot):
            copy.start()

    @pl.loop(0, slots)
    def _(slot):
        for copy in copies(slot):
            copy.wait()


def pick_pages(chosen, key_pool, value_pool):
    slots = chosen.shape[0]
    _, page, width = key_pool.shape
    return pl.pallas_call(
        pick_kernel,
        out_shape=jax.ShapeDtypeStruct((slots, 2 * page, width), BF16),
        in_specs=[SMEM_SPEC, ANY_SPEC, ANY_SPEC],
        out_specs=VMEM_SPEC,
        scratch_shapes=[pltpu.SemaphoreType.DMA((2, slots))],
        compiler_params=params(16),
        name="pick_pages",
    )(chosen, key_pool, value_pool)


def row_sums(values):
    squares = values * values
    folded = squares[:, :128]
    for start in range(128, values.shape[1], 128):
        folded = folded + squares[:, start : start + 128]
    return jnp.sum(folded.T, axis=0, keepdims=True)


def qkv_kernel(count, order, *refs):
    blocks = refs[:count]
    wq, wk, wv, q_out, k_out, v_out, stat = refs[count:]
    depth = blocks[0].shape[1]
    rows = blocks[0].shape[0]
    tile = 256
    for start in range(0, rows, tile):
        here = pl.ds(start, tile)
        sums = [None, None, None]
        for at in range(count):
            x = blocks[at][here, :]
            span = pl.ds(pl.multiple_of(order[at] * depth, depth), depth)
            for which, weight in enumerate((wq, wk, wv)):
                term = jnp.dot(x, weight[span, :], preferred_element_type=F32)
                sums[which] = term if at == 0 else sums[which] + term
        q_out[here, :] = sums[0]
        k_out[here, :] = sums[1]
        v_out[here, :] = sums[2].astype(BF16)
        stat[0:1, here] = row_sums(sums[0])
        stat[1:2, here] = row_sums(sums[1])


def qkv(order, blocks, wq, wk, wv):
    rows, depth = blocks[0].shape
    columns = wq.shape[1]
    return pl.pallas_call(
        functools.partial(qkv_kernel, len(blocks)),
        out_shape=(
            jax.ShapeDtypeStruct((rows, columns), F32),
            jax.ShapeDtypeStruct((rows, columns), F32),
            jax.ShapeDtypeStruct((rows, columns), BF16),
            jax.ShapeDtypeStruct((2, rows), F32),
        ),
        in_specs=[SMEM_SPEC] + [VMEM_SPEC] * (len(blocks) + 3),
        out_specs=(VMEM_SPEC,) * 4,
        compiler_params=params(32),
        cost_estimate=cost(2 * rows * depth * len(blocks) * 3 * columns, 9 << 20),
        name="qkv",
    )(order, *blocks, wq, wk, wv)


def down_rows(line):
    return jnp.broadcast_to(line, (128, line.shape[1])).T


def rope_kernel(full, q, k, stat, q_gain, k_gain, cosine, sine, q_out, k_out):
    tile = 256
    for start in range(0, q.shape[0], tile):
        here = pl.ds(start, tile)
        cos = cosine[here, :]
        sin = sine[here, :]
        for which, (source, gain, out) in enumerate(((q, q_gain, q_out), (k, k_gain, k_out))):
            scale = lax.rsqrt(down_rows(stat[which : which + 1, here]) / full + EPSILON)
            for column in range(0, source.shape[1], HEAD_DIM):
                span = pl.ds(column, HEAD_DIM)
                value = source[here, span] * scale * gain[0:1, span].astype(F32)
                turned = value * cos + pltpu.roll(value, HEAD_DIM // 2, 1) * sin
                out[here, span] = turned.astype(BF16)


def rope(full, q, k, stat, q_gain, k_gain, cosine, sine):
    shape = jax.ShapeDtypeStruct(q.shape, BF16)
    return pl.pallas_call(
        functools.partial(rope_kernel, full),
        out_shape=(shape, shape),
        in_specs=[VMEM_SPEC] * 7,
        out_specs=(VMEM_SPEC, VMEM_SPEC),
        compiler_params=params(16),
        cost_estimate=cost(20 * q.size, 4 << 20),
        name="rope",
    )(q, k, stat, q_gain, k_gain, cosine, sine)


def attend_kernel(query, new_k, new_v, pages, bias, out, scores, weights):
    tile = 256
    rows = query.shape[0]
    slots = pages.shape[0]
    page = pages.shape[1] // 2
    group = 4
    span = group * page
    cached = slots * page
    factor = HEAD_DIM**-0.5
    contract = (((1,), (1,)), ((), ()))
    for column in range(0, query.shape[1], HEAD_DIM):
        head = slice(column, column + HEAD_DIM)
        for start in range(0, rows, tile):
            q = query[start : start + tile, head]
            fresh = start + tile
            top = None
            for at in range(0, slots, group):
                k = pages[at : at + group, :page, head].reshape(span, HEAD_DIM)
                s = lax.dot_general(q, k, contract, preferred_element_type=F32) * factor
                s = s + bias[0:1, at * page : at * page + span]
                scores[:, at * page : at * page + span] = s
                part = s[:, :128]
                for lane in range(128, span, 128):
                    part = jnp.maximum(part, s[:, lane : lane + 128])
                top = part if top is None else jnp.maximum(top, part)
            for low in range(0, fresh, tile):
                k = new_k[low : low + tile, head]
                s = lax.dot_general(q, k, contract, preferred_element_type=F32) * factor
                if low == start:
                    row = lax.broadcasted_iota(jnp.int32, s.shape, 0)
                    col = lax.broadcasted_iota(jnp.int32, s.shape, 1)
                    s = jnp.where(row >= col, s, NEG)
                scores[:, cached + low : cached + low + tile] = s
                for lane in range(0, tile, 128):
                    top = jnp.maximum(top, s[:, lane : lane + 128])
            peak = jnp.max(top, axis=1, keepdims=True)
            total = None
            result = None
            for at in range(0, slots, group):
                raised = jnp.exp(scores[:, at * page : at * page + span] - peak)
                for lane in range(0, span, 128):
                    part = raised[:, lane : lane + 128]
                    total = part if total is None else total + part
                v = pages[at : at + group, page:, head].reshape(span, HEAD_DIM)
                term = jnp.dot(raised.astype(BF16), v, preferred_element_type=F32)
                result = term if result is None else result + term
            for low in range(0, fresh, tile):
                raised = jnp.exp(scores[:, cached + low : cached + low + tile] - peak)
                for lane in range(0, tile, 128):
                    total = total + raised[:, lane : lane + 128]
                term = jnp.dot(
                    raised.astype(BF16), new_v[low : low + tile, head], preferred_element_type=F32
                )
                result = result + term
            total = jnp.sum(total, axis=1, keepdims=True)
            out[start : start + tile, head] = (result / total).astype(BF16)


def attend(query, new_k, new_v, pages, bias):
    rows, columns = query.shape
    keys = bias.shape[1] + rows
    return pl.pallas_call(
        attend_kernel,
        out_shape=jax.ShapeDtypeStruct((rows, columns), BF16),
        in_specs=[VMEM_SPEC] * 5,
        out_specs=VMEM_SPEC,
        scratch_shapes=[pltpu.VMEM((256, keys), F32), pltpu.VMEM((8, 128), BF16)],
        compiler_params=params(40),
        cost_estimate=cost(4 * rows * keys * columns, 6 << 20),
        name="attend",
    )(query, new_k, new_v, pages, bias)


def project_kernel(count, order, *refs):
    blocks = refs[:count]
    weight, out, stat = refs[count:]
    rows, depth = blocks[0].shape
    tile = 256
    for start in range(0, rows, tile):
        here = pl.ds(start, tile)
        total = None
        for at in range(count):
            span = pl.ds(pl.multiple_of(order[at] * depth, depth), depth)
            term = jnp.dot(blocks[at][here, :], weight[span, :], preferred_element_type=F32)
            term = term.astype(BF16).astype(F32)
            total = term if at == 0 else total + term
        out[here, :] = total
        stat[0:1, here] = row_sums(total)


def project(order, blocks, weight):
    rows, depth = blocks[0].shape
    columns = weight.shape[1]
    return pl.pallas_call(
        functools.partial(project_kernel, len(blocks)),
        out_shape=(
            jax.ShapeDtypeStruct((rows, columns), F32),
            jax.ShapeDtypeStruct((1, rows), F32),
        ),
        in_specs=[SMEM_SPEC] + [VMEM_SPEC] * (len(blocks) + 1),
        out_specs=(VMEM_SPEC, VMEM_SPEC),
        compiler_params=params(24),
        cost_estimate=cost(2 * rows * depth * len(blocks) * columns, 5 << 20),
        name="project",
    )(order, *blocks, weight)


def finish_kernel(full, tokens, summed, stat, gain, out):
    tile = 256
    for start in range(0, tokens.shape[0], tile):
        here = pl.ds(start, tile)
        scale = lax.rsqrt(down_rows(stat[0:1, here]) / full + EPSILON)
        for column in range(0, tokens.shape[1], 128):
            span = pl.ds(column, 128)
            normed = summed[here, span] * scale
            value = tokens[here, span].astype(F32) + normed * gain[0:1, span].astype(F32)
            out[here, span] = value.astype(BF16)


def finish(full, tokens, summed, stat, gain):
    return pl.pallas_call(
        functools.partial(finish_kernel, full),
        out_shape=jax.ShapeDtypeStruct(tokens.shape, BF16),
        in_specs=[VMEM_SPEC] * 4,
        out_specs=VMEM_SPEC,
        compiler_params=params(16),
        name="finish",
    )(tokens, summed, stat, gain)


def ring_gather(block, size):
    right = [(i, (i + 1) % size) for i in range(size)]
    left = [(i, (i - 1) % size) for i in range(size)]
    found = [block]
    forward = backward = block
    for _ in range((size - 1) // 2):
        forward = lax.ppermute(forward, "tp", right)
        backward = lax.ppermute(backward, "tp", left)
        found += [forward, backward]
    half = block.shape[0] // 2
    far_a = lax.ppermute(forward[:half], "tp", right)
    far_b = lax.ppermute(backward[half:], "tp", left)
    return found + [jnp.concatenate([far_a, far_b], 0)]


def ring_order(size):
    me = lax.axis_index("tp")
    steps = [0]
    for step in range(1, (size - 1) // 2 + 1):
        steps += [-step, step]
    steps.append(size // 2)
    return (me + jnp.array(steps, jnp.int32) + size) % size


def body(
    tokens,
    q_weight,
    k_weight,
    v_weight,
    o_weight,
    q_gain,
    k_gain,
    post_gain,
    key_pool,
    value_pool,
    cache_len,
    page_table,
):
    _, block_len, feature_part = tokens.shape
    columns = q_weight.shape[1]
    owner = lax.axis_index("req")
    owners = lax.axis_size("req")
    size = lax.axis_size("tp")
    full = columns * size
    flat = tokens.reshape(block_len, feature_part)
    pool_dev, page_len, _ = key_pool.shape

    valid = page_table >= 0
    source = jnp.where(valid, page_table // pool_dev, -1)
    local = jnp.where(valid, page_table % pool_dev, 0)
    chosen = jnp.sum(jnp.where(source == owner, local, 0), 1)
    length = lax.dynamic_index_in_dim(cache_len, owner, 0, keepdims=False)
    mine = lax.dynamic_index_in_dim(source, owner, 0, keepdims=False)
    left = length - page_len * jnp.arange(mine.shape[0], dtype=jnp.int32)
    held = jnp.sum(
        jnp.where(mine[None, :] == jnp.arange(owners, dtype=jnp.int32)[:, None], left[None, :], 0), 1
    )
    bias = jnp.where(jnp.arange(page_len, dtype=jnp.int32)[None, :] < held[:, None], 0.0, NEG)
    bias = bias.astype(F32).reshape(1, owners * page_len)

    outgoing = pick_pages(chosen, key_pool, value_pool)
    arrived = lax.all_to_all(outgoing, "req", split_axis=0, concat_axis=0, tiled=True)

    order = ring_order(size)
    blocks = ring_gather(flat, size)
    q_proj, k_proj, new_values, stat = qkv(order, blocks, q_weight, k_weight, v_weight)
    stat = lax.psum(stat, "tp")

    half = HEAD_DIM // 2
    freqs = jnp.power(jnp.float32(ROPE_BASE), -jnp.arange(half, dtype=F32) * 2.0 / HEAD_DIM)
    positions = (length + jnp.arange(block_len, dtype=jnp.int32)).astype(F32)
    angles = positions[:, None] * freqs
    cosine = jnp.cos(angles)
    sine = jnp.sin(angles)
    cosine = jnp.concatenate([cosine, cosine], 1)
    sine = jnp.concatenate([-sine, sine], 1)
    query, new_keys = rope(
        full, q_proj, k_proj, stat, q_gain[None], k_gain[None], cosine, sine
    )

    o_columns = lax.all_to_all(o_weight, "tp", split_axis=1, concat_axis=0, tiled=True)

    attended = attend(query, new_keys, new_values, arrived, bias)
    parts = ring_gather(attended, size)
    summed, squares = project(order, parts, o_columns)
    squares = lax.psum(squares, "tp")
    mixed = finish(full, flat, summed, squares, post_gain[None])
    return (mixed[None], new_keys[None], new_values[None])


def solution(mesh):
    placed = (
        P("req", None, "tp"),
        P(None, "tp"),
        P(None, "tp"),
        P(None, "tp"),
        P("tp", None),
        P("tp"),
        P("tp"),
        P("tp"),
        P("req", None, "tp"),
        P("req", None, "tp"),
        P(),
        P(),
    )
    return jax.shard_map(
        body,
        mesh=mesh,
        in_specs=placed,
        out_specs=(P("req", None, "tp"), P("req", None, "tp"), P("req", None, "tp")),
        check_vma=False,
    )
```

```python
import functools

import jax
import jax.numpy as jnp
from jax import lax
from jax.experimental import pallas as pl
from jax.experimental.pallas import tpu as pltpu
from jax.sharding import PartitionSpec as P


HEAD_DIM = 128
EPSILON = 1e-06
ROPE_BASE = 500000.0
NEG = -1e30
F32 = jnp.float32
BF16 = jnp.bfloat16
VMEM_SPEC = pl.BlockSpec(memory_space=pltpu.VMEM)
SMEM_SPEC = pl.BlockSpec(memory_space=pltpu.SMEM)
HBM_SPEC = pl.BlockSpec(memory_space=pltpu.HBM)


def cost(flops, moved):
    return pl.CostEstimate(flops=flops, bytes_accessed=moved, transcendentals=0)


def params(mib):
    return pltpu.CompilerParams(vmem_limit_bytes=mib << 20)


def pick_kernel(
    chosen, place, lengths, freqs, key_pool, value_pool, out, cosine, sine, held, sem
):
    slots, page = out.shape[0], key_pool.shape[1]
    group = 8
    for slot in range(slots):
        index = chosen[slot]
        for part, pool in enumerate((key_pool, value_pool)):
            pltpu.make_async_copy(
                pool.at[index], held.at[slot, pl.ds(part * page, page)], sem.at[0, slot // group]
            ).start()

    length = lengths[place[0]]
    rows = cosine.shape[0]
    tile = 256
    for start in range(0, rows, tile):
        row = lax.broadcasted_iota(jnp.int32, (tile, 128), 0)
        lane = lax.broadcasted_iota(jnp.int32, (tile, 128), 1)
        angles = (row + (length + start)).astype(F32) * freqs[...]
        cosine[start : start + tile, :] = jnp.cos(angles)
        turned = jnp.sin(angles)
        sine[start : start + tile, :] = jnp.where(lane < 64, -turned, turned)

    leaving = []
    for at in range(0, slots, group):
        here = pl.ds(at, group)
        pltpu.make_async_copy(out.at[here], held.at[here], sem.at[0, at // group]).wait()
        leaving.append(pltpu.make_async_copy(held.at[here], out.at[here], sem.at[1, at // group]))
        leaving[-1].start()
    for copy in leaving:
        copy.wait()


def pick_pages(rows, chosen, place, lengths, freqs, key_pool, value_pool):
    slots = chosen.shape[0]
    _, page, width = key_pool.shape
    return pl.pallas_call(
        pick_kernel,
        out_shape=(
            jax.ShapeDtypeStruct((slots, 2 * page, width), BF16),
            jax.ShapeDtypeStruct((rows, HEAD_DIM), F32),
            jax.ShapeDtypeStruct((rows, HEAD_DIM), F32),
        ),
        in_specs=[SMEM_SPEC] * 3 + [VMEM_SPEC, HBM_SPEC, HBM_SPEC],
        out_specs=(HBM_SPEC, VMEM_SPEC, VMEM_SPEC),
        scratch_shapes=[
            pltpu.VMEM((slots, 2 * page, width), BF16),
            pltpu.SemaphoreType.DMA((2, slots // 8)),
        ],
        compiler_params=params(62),
        name="pick_pages",
    )(chosen, place, lengths, freqs, key_pool, value_pool)


def row_sums(values):
    squares = values * values
    folded = squares[:, :128]
    for start in range(128, values.shape[1], 128):
        folded = folded + squares[:, start : start + 128]
    return jnp.sum(folded.T, axis=0, keepdims=True)


def qkv_kernel(count, parts, order, *refs):
    blocks = refs[: count * parts]
    wq, wk, wv, q_out, k_out, v_out, stat, x, w, sem, w_sem = refs[count * parts :]
    depth = x.shape[2]
    rows = x.shape[1]
    piece = rows // parts

    def weight_copy(which, source):
        return pltpu.make_async_copy(source, w.at[which], w_sem.at[which])

    def block_copy(at, part):
        return pltpu.make_async_copy(
            blocks[at * parts + part], x.at[at, pl.ds(part * piece, piece)], sem.at[at, part]
        )

    weight_copy(0, wq).start()
    for at in range(count):
        block_copy(at, 0).start()
    weight_copy(1, wk).start()
    weight_copy(2, wv).start()
    for part in range(1, parts):
        for at in range(count):
            block_copy(at, part).start()
    tile = 256
    ready = 0
    for start in range(0, rows, tile):
        here = slice(start, start + tile)
        needed = -(-(start + tile) // piece)
        for which, (source, out) in enumerate(((wq, q_out), (wk, k_out), (wv, v_out))):
            if start == 0:
                weight_copy(which, source).wait()
            total = None
            for at in range(count):
                for part in range(ready, needed):
                    block_copy(at, part).wait()
                span = pl.ds(pl.multiple_of(order[at] * depth, depth), depth)
                term = jnp.dot(x[at, here, :], w[which, span, :], preferred_element_type=F32)
                total = term if total is None else total + term
            ready = needed
            out[here, :] = total.astype(out.dtype)
            if which < 2:
                stat[which : which + 1, here] = row_sums(total)


def qkv(order, blocks, wq, wk, wv):
    count = len(blocks)
    parts = len(blocks[0])
    piece, depth = blocks[0][0].shape
    rows = piece * parts
    columns = wq.shape[1]
    return pl.pallas_call(
        functools.partial(qkv_kernel, count, parts),
        out_shape=(
            jax.ShapeDtypeStruct((rows, columns), F32),
            jax.ShapeDtypeStruct((rows, columns), F32),
            jax.ShapeDtypeStruct((rows, columns), BF16),
            jax.ShapeDtypeStruct((2, rows), F32),
        ),
        in_specs=[SMEM_SPEC] + [HBM_SPEC] * (count * parts + 3),
        out_specs=(VMEM_SPEC,) * 4,
        scratch_shapes=[
            pltpu.VMEM((count, rows, depth), BF16),
            pltpu.VMEM((3, wq.shape[0], columns), BF16),
            pltpu.SemaphoreType.DMA((count, parts)),
            pltpu.SemaphoreType.DMA((3,)),
        ],
        compiler_params=params(62),
        cost_estimate=cost(2 * rows * depth * count * 3 * columns, 9 << 20),
        name="qkv",
    )(order, *[piece for block in blocks for piece in block], wq, wk, wv)


def down_rows(line):
    return jnp.broadcast_to(line, (128, line.shape[1])).T


def attend_kernel(
    full,
    place,
    lengths,
    page_table,
    stat,
    q_gain,
    k_gain,
    q_hbm,
    k_hbm,
    v_hbm,
    cos_hbm,
    sin_hbm,
    pages_hbm,
    out,
    keys_out,
    raw,
    table,
    query,
    new_k,
    new_v,
    pages,
    ones,
    scores,
    counts,
    sem,
    page_sem,
):
    tile = 256
    slots = pages.shape[0]
    rows, columns = query.shape
    page = pages.shape[1] // 2
    group = 8
    span = group * page
    cached = slots * page
    factor = HEAD_DIM**-0.5 * 1.4426950408889634
    contract = (((1,), (1,)), ((), ()))
    small = [
        pltpu.make_async_copy(source, held, sem.at[at])
        for at, (source, held) in enumerate(
            (
                (q_hbm, raw.at[0]),
                (cos_hbm, table.at[0]),
                (sin_hbm, table.at[1]),
                (k_hbm, raw.at[1]),
                (v_hbm, new_v),
            )
        )
    ]
    for copy in small:
        copy.start()
    parts = [
        pltpu.make_async_copy(
            pages_hbm.at[pl.ds(at, group)], pages.at[pl.ds(at, group)], page_sem.at[at // group]
        )
        for at in range(0, slots, group)
    ]
    for copy in parts:
        copy.start()

    owner = place[0]
    length = lengths[owner]
    ones[...] = jnp.ones(ones.shape, BF16)

    @pl.loop(0, slots)
    def _(slot):
        counts[slot] = 0

    @pl.loop(0, page_table.shape[1])
    def _(at):
        entry = page_table[owner, at]

        @pl.when(entry >= 0)
        def _():
            counts[lax.div(entry, slots)] = length - at * page

    for which, gain in enumerate((q_gain, k_gain)):
        for copy in small[:3] if which == 0 else small[3:4]:
            copy.wait()
        for start in range(0, rows, tile):
            here = slice(start, start + tile)
            scale = lax.rsqrt(down_rows(stat[which : which + 1, here]) / full + EPSILON)
            for low in range(0, columns, HEAD_DIM):
                lanes = slice(low, low + HEAD_DIM)
                value = raw[which, here, lanes] * scale * gain[0:1, lanes].astype(F32)
                turned = value * table[0, here, :]
                turned = turned + pltpu.roll(value, HEAD_DIM // 2, 1) * table[1, here, :]
                turned = turned.astype(BF16)
                if which == 0:
                    query[here, lanes] = turned
                else:
                    new_k[here, lanes] = turned
                    keys_out[here, lanes] = turned
    small[4].wait()
    for copy in parts:
        copy.wait()

    first = lax.div(page_table[owner, 0], slots)
    key = jnp.broadcast_to(pages[first, 0:1, :], (page, columns))

    @pl.loop(0, slots)
    def _(slot):
        exist = counts[slot]

        @pl.when(exist < page)
        def _():
            for low in range(0, columns, 128):
                lanes = slice(low, low + 128)
                row = lax.broadcasted_iota(jnp.int32, (page, 128), 0)
                keep = row < exist
                kept = pages[slot, :page, lanes].astype(F32)
                spare = key[:, lanes].astype(F32)
                pages[slot, :page, lanes] = jnp.where(keep, kept, spare).astype(BF16)
                value = pages[slot, page:, lanes].astype(F32)
                pages[slot, page:, lanes] = jnp.where(keep, value, 0.0).astype(BF16)
                if low == 0:
                    ones[slot] = jnp.where(keep, 1.0, 0.0).astype(BF16)

    one = jnp.ones((tile, HEAD_DIM), BF16)
    for column in range(0, columns, HEAD_DIM):
        head = slice(column, column + HEAD_DIM)
        for start in range(0, rows, tile):
            q = query[start : start + tile, head]
            fresh = start + tile
            top = None
            for at in range(0, slots, group):
                k = pages[at : at + group, :page, head].reshape(span, HEAD_DIM)
                s = lax.dot_general(q, k, contract, preferred_element_type=F32)
                scores[:, at * page : at * page + span] = s
                for lane in range(0, span, 128):
                    part = s[:, lane : lane + 128]
                    top = part if top is None else jnp.maximum(top, part)
            for low in range(0, fresh, tile):
                k = new_k[low : low + tile, head]
                s = lax.dot_general(q, k, contract, preferred_element_type=F32)
                if low == start:
                    row = lax.broadcasted_iota(jnp.int32, s.shape, 0)
                    col = lax.broadcasted_iota(jnp.int32, s.shape, 1)
                    s = jnp.where(row >= col, s, NEG)
                scores[:, cached + low : cached + low + tile] = s
                for lane in range(0, tile, 128):
                    top = jnp.maximum(top, s[:, lane : lane + 128])
            peak = jnp.max(top, axis=1, keepdims=True)
            result = None
            for at in range(0, slots, group):
                raised = jnp.exp2((scores[:, at * page : at * page + span] - peak) * factor)
                v = jnp.concatenate(
                    [
                        pages[at : at + group, page:, head].reshape(span, HEAD_DIM),
                        ones[at : at + group].reshape(span, HEAD_DIM),
                    ],
                    1,
                )
                term = jnp.dot(raised.astype(BF16), v, preferred_element_type=F32)
                result = term if result is None else result + term
            for low in range(0, fresh, tile):
                raised = jnp.exp2(
                    (scores[:, cached + low : cached + low + tile] - peak) * factor
                )
                v = jnp.concatenate([new_v[low : low + tile, head], one], 1)
                result = result + jnp.dot(raised.astype(BF16), v, preferred_element_type=F32)
            result = result[:, :HEAD_DIM] / result[:, HEAD_DIM:]
            out[start : start + tile, head] = result.astype(BF16)


def attend(
    full, place, lengths, page_table, stat, q_gain, k_gain, q_proj, k_proj, new_v, cosine, sine, pages
):
    rows, columns = q_proj.shape
    slots, both, _ = pages.shape
    keys = slots * both // 2 + rows
    held = pltpu.VMEM((rows, columns), BF16)
    shape = jax.ShapeDtypeStruct((rows, columns), BF16)
    return pl.pallas_call(
        functools.partial(attend_kernel, full),
        out_shape=(shape, shape),
        in_specs=[SMEM_SPEC] * 3 + [VMEM_SPEC] * 3 + [HBM_SPEC] * 6,
        out_specs=(VMEM_SPEC, VMEM_SPEC),
        scratch_shapes=[
            pltpu.VMEM((2, rows, columns), F32),
            pltpu.VMEM((2, rows, HEAD_DIM), F32),
            held,
            held,
            held,
            pltpu.VMEM((slots, both, columns), BF16),
            pltpu.VMEM((slots, both // 2, HEAD_DIM), BF16),
            pltpu.VMEM((256, keys), F32),
            pltpu.SMEM((slots,), jnp.int32),
            pltpu.SemaphoreType.DMA((5,)),
            pltpu.SemaphoreType.DMA((slots,)),
        ],
        compiler_params=params(62),
        cost_estimate=cost(4 * rows * keys * columns, 9 << 20),
        name="attend",
    )(place, lengths, page_table, stat, q_gain, k_gain, q_proj, k_proj, new_v, cosine, sine, pages)


def project_kernel(full, order, *refs):
    heads, *blocks, near_half, far_half, out, held, weight, total, sem = refs
    count = len(blocks) + 1
    depth = heads.shape[1]
    share = total.shape[0]
    half = depth // 2
    core = order[count]
    copies = [
        pltpu.make_async_copy(block, weight.at[at], sem.at[at]) for at, block in enumerate(blocks)
    ]
    for at, (source, offset) in enumerate(((near_half, core), (far_half, 1 - core))):
        rows = pl.ds(pl.multiple_of(offset * half, half), half)
        copies.append(
            pltpu.make_async_copy(source, weight.at[count - 1, rows], sem.at[count - 1 + at])
        )
    load = pltpu.make_async_copy(heads, held, sem.at[count + 1])
    load.start()
    for copy in copies:
        copy.start()
    load.wait()
    wide = 1024
    for at in range(count):
        copies[at].wait()
        if at == count - 1:
            copies[count].wait()
        rows = pl.ds(pl.multiple_of(order[at] * share, share), share)
        x = held[rows, :]
        for start in range(0, full, wide):
            span = slice(start, start + wide)
            term = jnp.dot(x, weight[at, :, span], preferred_element_type=F32)
            total[:, span] = term if at == 0 else total[:, span] + term
    value = total[...]
    scale = lax.rsqrt(jnp.sum(value * value, axis=1, keepdims=True) / full + EPSILON)
    for at in range(count):
        normed = total[:, at * depth : (at + 1) * depth] * scale
        out[at * share : (at + 1) * share, :] = normed.astype(BF16)


def project(order, heads, blocks, near_half, far_half):
    rows, depth = heads.shape
    count = len(blocks) + 1
    full = blocks[0].shape[1]
    share = rows // count
    return pl.pallas_call(
        functools.partial(project_kernel, full),
        out_shape=jax.ShapeDtypeStruct((rows, depth), BF16),
        in_specs=[SMEM_SPEC] + [HBM_SPEC] * (count + 2),
        out_specs=VMEM_SPEC,
        scratch_shapes=[
            pltpu.VMEM((rows, depth), BF16),
            pltpu.VMEM((count, depth, full), BF16),
            pltpu.VMEM((share, full), F32),
            pltpu.SemaphoreType.DMA((count + 2,)),
        ],
        compiler_params=params(62),
        cost_estimate=cost(2 * rows * depth * full, 9 << 20),
        name="project",
    )(order, heads, *blocks, near_half, far_half)


def ring_gather(block, size, parts):
    right = [(i, (i + 1) % size) for i in range(size)]
    left = [(i, (i - 1) % size) for i in range(size)]
    piece = block.shape[0] // parts
    pieces = [block[at * piece : (at + 1) * piece] for at in range(parts)]
    found = [pieces]
    forward, backward = list(pieces), list(pieces)
    for _ in range((size - 1) // 2):
        for at in range(parts):
            forward[at] = lax.ppermute(forward[at], "tp", right)
            backward[at] = lax.ppermute(backward[at], "tp", left)
        found += [list(forward), list(backward)]
    far = [
        lax.ppermute(forward[at], "tp", right)
        if at < parts // 2
        else lax.ppermute(backward[at], "tp", left)
        for at in range(parts)
    ]
    return found + [far]


def ring_order(size):
    me = lax.axis_index("tp")
    steps = [0]
    for step in range(1, (size - 1) // 2 + 1):
        steps += [-step, step]
    steps.append(size // 2)
    return (me + jnp.array(steps, jnp.int32) + size) % size


def weight_moves(owners, size):
    onward = []
    swap = []
    for r in range(owners):
        for t in range(size):
            to = (t + (1 if r % 2 == 0 else -1)) % size
            onward.append((r * size + t, r * size + to))
            swap.append((r * size + t, (r ^ 1) * size + t))
    return onward, swap


def after(value, *others):
    return lax.optimization_barrier((value, *others))[0]


def body(
    tokens,
    q_weight,
    k_weight,
    v_weight,
    o_weight,
    q_gain,
    k_gain,
    post_gain,
    key_pool,
    value_pool,
    cache_len,
    page_table,
):
    _, block_len, feature_part = tokens.shape
    columns = q_weight.shape[1]
    owner = lax.axis_index("req")
    owners = lax.axis_size("req")
    size = lax.axis_size("tp")
    full = columns * size
    flat = tokens.reshape(block_len, feature_part)
    pool_dev, _, _ = key_pool.shape

    valid = page_table >= 0
    source = jnp.where(valid, page_table // pool_dev, -1)
    local = jnp.where(valid, page_table % pool_dev, 0)
    chosen = jnp.sum(jnp.where(source == owner, local, 0), 1)
    half = HEAD_DIM // 2
    freqs = jnp.power(jnp.float32(ROPE_BASE), -jnp.arange(half, dtype=F32) * 2.0 / HEAD_DIM)
    freqs = jnp.concatenate([freqs, freqs])[None]
    outgoing, cosine, sine = pick_pages(
        block_len, chosen, owner[None], cache_len, freqs, key_pool, value_pool
    )
    arrived = lax.all_to_all(outgoing, "req", split_axis=0, concat_axis=0, tiled=True)

    axes = ("req", "tp")
    onward, swap = weight_moves(owners, size)

    def move(value, pairs):
        return lax.ppermute(value, axes, pairs)

    order = ring_order(size)
    blocks = ring_gather(after(flat, outgoing), size, 2)
    o_1 = move(o_weight, onward)
    o_1 = after(o_1, *(piece for block in blocks[-3:] for piece in block))
    o_2 = move(o_1, onward)
    s_1 = move(o_1, swap)
    q_proj, k_proj, new_values, stat = qkv(order, blocks, q_weight, k_weight, v_weight)
    stat = lax.psum(stat, "tp")
    o_2 = after(o_2, stat)
    o_3 = move(o_2, onward)
    s_2 = move(o_2, swap)
    attended, new_keys = attend(
        full,
        owner[None],
        cache_len,
        page_table,
        stat,
        q_gain[None],
        k_gain[None],
        q_proj,
        k_proj,
        new_values,
        cosine,
        sine,
        arrived,
    )
    core = owner % 2
    share = o_weight.shape[0] // 2
    o_4 = move(lax.dynamic_slice_in_dim(o_3, core * share, share, 0), onward)
    s_3 = move(o_3, swap)
    s_4 = move(o_4, swap)
    heads = lax.all_to_all(attended, "tp", split_axis=0, concat_axis=0, tiled=True)

    me = lax.axis_index("tp")
    turn = 1 - 2 * core
    steps = [0]
    for step in range(1, (size - 1) // 2 + 1):
        steps += [-step, step]
    steps.append(size // 2)
    weight_order = (me + turn * jnp.array(steps, jnp.int32) + size) % size
    weight_order = jnp.concatenate([weight_order, core[None].astype(jnp.int32)])
    normed = project(
        weight_order, heads, [o_weight, o_1, s_1, o_2, s_2, o_3, s_3], o_4, s_4
    )
    normed = lax.all_to_all(normed, "tp", split_axis=0, concat_axis=0, tiled=True)
    mixed = flat.astype(F32) + normed.astype(F32) * post_gain.astype(F32)
    return (mixed.astype(BF16)[None], new_keys[None], new_values[None])


def solution(mesh):
    placed = (
        P("req", None, "tp"),
        P(None, "tp"),
        P(None, "tp"),
        P(None, "tp"),
        P("tp", None),
        P("tp"),
        P("tp"),
        P("tp"),
        P("req", None, "tp"),
        P("req", None, "tp"),
        P(),
        P(),
    )

    return jax.shard_map(
        body,
        mesh=mesh,
        in_specs=placed,
        out_specs=(P("req", None, "tp"), P("req", None, "tp"), P("req", None, "tp")),
        check_vma=False,
    )
```

```python
import functools

import jax
import jax.numpy as jnp
from jax import lax
from jax.experimental import pallas as pl
from jax.experimental.pallas import tpu as pltpu
from jax.sharding import PartitionSpec as P


HEAD_DIM = 128
EPSILON = 1e-06
ROPE_BASE = 500000.0
NEG = -1e30
F32 = jnp.float32
BF16 = jnp.bfloat16
VMEM_SPEC = pl.BlockSpec(memory_space=pltpu.VMEM)
SMEM_SPEC = pl.BlockSpec(memory_space=pltpu.SMEM)
HBM_SPEC = pl.BlockSpec(memory_space=pltpu.HBM)


def cost(flops, moved):
    return pl.CostEstimate(flops=flops, bytes_accessed=moved, transcendentals=0)


def params(mib):
    return pltpu.CompilerParams(vmem_limit_bytes=mib << 20)


def pick_kernel(
    chosen, place, lengths, freqs, key_pool, value_pool, out, cosine, sine, held, sem
):
    slots, page = out.shape[0], key_pool.shape[1]
    group = 8
    for slot in range(slots):
        index = chosen[slot]
        for part, pool in enumerate((key_pool, value_pool)):
            pltpu.make_async_copy(
                pool.at[index], held.at[slot, pl.ds(part * page, page)], sem.at[0, slot // group]
            ).start()

    length = lengths[place[0]]
    rows = cosine.shape[0]
    tile = 256
    for start in range(0, rows, tile):
        row = lax.broadcasted_iota(jnp.int32, (tile, 128), 0)
        lane = lax.broadcasted_iota(jnp.int32, (tile, 128), 1)
        angles = (row + (length + start)).astype(F32) * freqs[...]
        cosine[start : start + tile, :] = jnp.cos(angles)
        turned = jnp.sin(angles)
        sine[start : start + tile, :] = jnp.where(lane < 64, -turned, turned)

    leaving = []
    for at in range(0, slots, group):
        here = pl.ds(at, group)
        pltpu.make_async_copy(out.at[here], held.at[here], sem.at[0, at // group]).wait()
        leaving.append(pltpu.make_async_copy(held.at[here], out.at[here], sem.at[1, at // group]))
        leaving[-1].start()
    for copy in leaving:
        copy.wait()


def pick_pages(rows, chosen, place, lengths, freqs, key_pool, value_pool):
    slots = chosen.shape[0]
    _, page, width = key_pool.shape
    return pl.pallas_call(
        pick_kernel,
        out_shape=(
            jax.ShapeDtypeStruct((slots, 2 * page, width), BF16),
            jax.ShapeDtypeStruct((rows, HEAD_DIM), F32),
            jax.ShapeDtypeStruct((rows, HEAD_DIM), F32),
        ),
        in_specs=[SMEM_SPEC] * 3 + [VMEM_SPEC, HBM_SPEC, HBM_SPEC],
        out_specs=(HBM_SPEC, VMEM_SPEC, VMEM_SPEC),
        scratch_shapes=[
            pltpu.VMEM((slots, 2 * page, width), BF16),
            pltpu.SemaphoreType.DMA((2, slots // 8)),
        ],
        compiler_params=params(62),
        name="pick_pages",
    )(chosen, place, lengths, freqs, key_pool, value_pool)


def row_sums(values):
    squares = values * values
    folded = squares[:, :128]
    for start in range(128, values.shape[1], 128):
        folded = folded + squares[:, start : start + 128]
    return jnp.sum(folded.T, axis=0, keepdims=True)


def qkv_kernel(count, parts, order, *refs):
    blocks = refs[: count * parts]
    wq, wk, wv, q_out, k_out, v_out, stat, x, w, raw, values, sem, w_sem, out_sem = refs[
        count * parts :
    ]
    depth = x.shape[2]
    rows = x.shape[1]
    piece = rows // parts

    def weight_copy(which, source):
        return pltpu.make_async_copy(source, w.at[which], w_sem.at[which])

    def part_copy(at, part):
        return pltpu.make_async_copy(
            blocks[at * parts + part], x.at[at, pl.ds(part * piece, piece)], sem.at[part]
        )

    def part_wait(part):
        whole = x.at[:, pl.ds(part * piece, piece)]
        pltpu.make_async_copy(whole, whole, sem.at[part]).wait()

    weight_copy(0, wq).start()
    for at in range(count):
        part_copy(at, 0).start()
    weight_copy(1, wk).start()
    weight_copy(2, wv).start()
    for part in range(1, parts):
        for at in range(count):
            part_copy(at, part).start()
    tile = 256
    ready = 0
    leaving = []
    for start in range(0, rows, tile):
        here = slice(start, start + tile)
        needed = -(-(start + tile) // piece)
        for which, source in enumerate((wq, wk, wv)):
            if start == 0:
                weight_copy(which, source).wait()
            for part in range(ready, needed):
                part_wait(part)
            ready = needed
            total = None
            for at in range(count):
                span = pl.ds(pl.multiple_of(order[at] * depth, depth), depth)
                term = jnp.dot(x[at, here, :], w[which, span, :], preferred_element_type=F32)
                total = term if total is None else total + term
            if which < 2:
                raw[which, here, :] = total
                stat[which : which + 1, here] = row_sums(total)
                held, out = raw.at[which], (q_out, k_out)[which]
            else:
                values[here, :] = total.astype(BF16)
                held, out = values, v_out
            span = pl.ds(start, tile)
            leaving.append(
                pltpu.make_async_copy(
                    held.at[span], out.at[span], out_sem.at[which, start // tile]
                )
            )
            leaving[-1].start()
    for copy in leaving:
        copy.wait()


def qkv(order, blocks, wq, wk, wv):
    count = len(blocks)
    parts = len(blocks[0])
    piece, depth = blocks[0][0].shape
    rows = piece * parts
    columns = wq.shape[1]
    return pl.pallas_call(
        functools.partial(qkv_kernel, count, parts),
        out_shape=(
            jax.ShapeDtypeStruct((rows, columns), F32),
            jax.ShapeDtypeStruct((rows, columns), F32),
            jax.ShapeDtypeStruct((rows, columns), BF16),
            jax.ShapeDtypeStruct((2, rows), F32),
        ),
        in_specs=[SMEM_SPEC] + [HBM_SPEC] * (count * parts + 3),
        out_specs=(HBM_SPEC, HBM_SPEC, HBM_SPEC, VMEM_SPEC),
        scratch_shapes=[
            pltpu.VMEM((count, rows, depth), BF16),
            pltpu.VMEM((3, wq.shape[0], columns), BF16),
            pltpu.VMEM((2, rows, columns), F32),
            pltpu.VMEM((rows, columns), BF16),
            pltpu.SemaphoreType.DMA((parts,)),
            pltpu.SemaphoreType.DMA((3,)),
            pltpu.SemaphoreType.DMA((3, rows // 256)),
        ],
        compiler_params=params(62),
        cost_estimate=cost(2 * rows * depth * count * 3 * columns, 9 << 20),
        name="qkv",
    )(order, *[piece for block in blocks for piece in block], wq, wk, wv)


def down_rows(line):
    return jnp.broadcast_to(line, (128, line.shape[1])).T


def attend_kernel(
    full,
    place,
    lengths,
    page_table,
    stat,
    q_gain,
    k_gain,
    q_hbm,
    k_hbm,
    v_hbm,
    cos_hbm,
    sin_hbm,
    pages_hbm,
    out,
    keys_out,
    raw,
    table,
    query,
    new_k,
    new_v,
    pages,
    ones,
    scores,
    result_rows,
    counts,
    sem,
    page_sem,
    out_sem,
):
    tile = 256
    slots = pages.shape[0]
    rows, columns = query.shape
    page = pages.shape[1] // 2
    group = 8
    span = group * page
    cached = slots * page
    factor = HEAD_DIM**-0.5 * 1.4426950408889634
    contract = (((1,), (1,)), ((), ()))
    small = [
        pltpu.make_async_copy(source, held, sem.at[at])
        for at, (source, held) in enumerate(
            (
                (q_hbm, raw.at[0]),
                (cos_hbm, table.at[0]),
                (sin_hbm, table.at[1]),
                (k_hbm, raw.at[1]),
                (v_hbm, new_v),
            )
        )
    ]
    for copy in small:
        copy.start()
    parts = [
        pltpu.make_async_copy(
            pages_hbm.at[pl.ds(at, group)], pages.at[pl.ds(at, group)], page_sem.at[at // group]
        )
        for at in range(0, slots, group)
    ]
    for copy in parts:
        copy.start()

    owner = place[0]
    length = lengths[owner]
    ones[...] = jnp.ones(ones.shape, BF16)

    @pl.loop(0, slots)
    def _(slot):
        counts[slot] = 0

    @pl.loop(0, page_table.shape[1])
    def _(at):
        entry = page_table[owner, at]

        @pl.when(entry >= 0)
        def _():
            counts[lax.div(entry, slots)] = length - at * page

    for which, gain in enumerate((q_gain, k_gain)):
        for copy in small[:3] if which == 0 else small[3:4]:
            copy.wait()
        for start in range(0, rows, tile):
            here = slice(start, start + tile)
            scale = lax.rsqrt(down_rows(stat[which : which + 1, here]) / full + EPSILON)
            for low in range(0, columns, HEAD_DIM):
                lanes = slice(low, low + HEAD_DIM)
                value = raw[which, here, lanes] * scale * gain[lanes].astype(F32)[None]
                turned = value * table[0, here, :]
                turned = turned + pltpu.roll(value, HEAD_DIM // 2, 1) * table[1, here, :]
                turned = turned.astype(BF16)
                if which == 0:
                    query[here, lanes] = turned
                else:
                    new_k[here, lanes] = turned
    leaving = [pltpu.make_async_copy(new_k, keys_out, out_sem.at[0])]
    leaving[0].start()
    small[4].wait()
    for copy in parts:
        copy.wait()

    first = lax.div(page_table[owner, 0], slots)
    key = jnp.broadcast_to(pages[first, 0:1, :], (page, columns))

    @pl.loop(0, slots)
    def _(slot):
        exist = counts[slot]

        @pl.when(exist < page)
        def _():
            for low in range(0, columns, 128):
                lanes = slice(low, low + 128)
                row = lax.broadcasted_iota(jnp.int32, (page, 128), 0)
                keep = row < exist
                kept = pages[slot, :page, lanes].astype(F32)
                spare = key[:, lanes].astype(F32)
                pages[slot, :page, lanes] = jnp.where(keep, kept, spare).astype(BF16)
                value = pages[slot, page:, lanes].astype(F32)
                pages[slot, page:, lanes] = jnp.where(keep, value, 0.0).astype(BF16)
                if low == 0:
                    ones[slot] = jnp.where(keep, 1.0, 0.0).astype(BF16)

    one = jnp.ones((tile, HEAD_DIM), BF16)
    for column in range(0, columns, HEAD_DIM):
        head = slice(column, column + HEAD_DIM)
        for start in range(0, rows, tile):
            q = query[start : start + tile, head]
            fresh = start + tile
            top = None
            for at in range(0, slots, group):
                k = pages[at : at + group, :page, head].reshape(span, HEAD_DIM)
                s = lax.dot_general(q, k, contract, preferred_element_type=F32)
                scores[:, at * page : at * page + span] = s
                for lane in range(0, span, 128):
                    part = s[:, lane : lane + 128]
                    top = part if top is None else jnp.maximum(top, part)
            for low in range(0, fresh, tile):
                k = new_k[low : low + tile, head]
                s = lax.dot_general(q, k, contract, preferred_element_type=F32)
                if low == start:
                    row = lax.broadcasted_iota(jnp.int32, s.shape, 0)
                    col = lax.broadcasted_iota(jnp.int32, s.shape, 1)
                    s = jnp.where(row >= col, s, NEG)
                scores[:, cached + low : cached + low + tile] = s
                for lane in range(0, tile, 128):
                    top = jnp.maximum(top, s[:, lane : lane + 128])
            peak = jnp.max(top, axis=1, keepdims=True)
            result = None
            for at in range(0, slots, group):
                raised = jnp.exp2((scores[:, at * page : at * page + span] - peak) * factor)
                v = jnp.concatenate(
                    [
                        pages[at : at + group, page:, head].reshape(span, HEAD_DIM),
                        ones[at : at + group].reshape(span, HEAD_DIM),
                    ],
                    1,
                )
                term = jnp.dot(raised.astype(BF16), v, preferred_element_type=F32)
                result = term if result is None else result + term
            for low in range(0, fresh, tile):
                raised = jnp.exp2(
                    (scores[:, cached + low : cached + low + tile] - peak) * factor
                )
                v = jnp.concatenate([new_v[low : low + tile, head], one], 1)
                result = result + jnp.dot(raised.astype(BF16), v, preferred_element_type=F32)
            result = result[:, :HEAD_DIM] / result[:, HEAD_DIM:]
            result_rows[start : start + tile, head] = result.astype(BF16)
            if column + HEAD_DIM == columns:
                here = pl.ds(start, tile)
                leaving.append(
                    pltpu.make_async_copy(
                        result_rows.at[here], out.at[here], out_sem.at[1 + start // tile]
                    )
                )
                leaving[-1].start()
    for copy in leaving:
        copy.wait()


def attend(
    full, place, lengths, page_table, stat, q_gain, k_gain, q_proj, k_proj, new_v, cosine, sine, pages
):
    rows, columns = q_proj.shape
    slots, both, _ = pages.shape
    keys = slots * both // 2 + rows
    held = pltpu.VMEM((rows, columns), BF16)
    shape = jax.ShapeDtypeStruct((rows, columns), BF16)
    return pl.pallas_call(
        functools.partial(attend_kernel, full),
        out_shape=(shape, shape),
        in_specs=[SMEM_SPEC] * 3 + [VMEM_SPEC] * 3 + [HBM_SPEC] * 6,
        out_specs=(HBM_SPEC, HBM_SPEC),
        scratch_shapes=[
            pltpu.VMEM((2, rows, columns), F32),
            pltpu.VMEM((2, rows, HEAD_DIM), F32),
            held,
            held,
            held,
            pltpu.VMEM((slots, both, columns), BF16),
            pltpu.VMEM((slots, both // 2, HEAD_DIM), BF16),
            pltpu.VMEM((256, keys), F32),
            held,
            pltpu.SMEM((slots,), jnp.int32),
            pltpu.SemaphoreType.DMA((5,)),
            pltpu.SemaphoreType.DMA((slots,)),
            pltpu.SemaphoreType.DMA((1 + rows // 256,)),
        ],
        compiler_params=params(62),
        cost_estimate=cost(4 * rows * keys * columns, 9 << 20),
        name="attend",
    )(place, lengths, page_table, stat, q_gain, k_gain, q_proj, k_proj, new_v, cosine, sine, pages)


def project_kernel(full, order, *refs):
    heads, *blocks, near_half, far_half, out, held, weight, total, sem = refs
    count = len(blocks) + 1
    depth = heads.shape[1]
    share = total.shape[0]
    half = depth // 2
    core = order[count]
    copies = [
        pltpu.make_async_copy(block, weight.at[at], sem.at[at]) for at, block in enumerate(blocks)
    ]
    for at, (source, offset) in enumerate(((near_half, core), (far_half, 1 - core))):
        rows = pl.ds(pl.multiple_of(offset * half, half), half)
        copies.append(
            pltpu.make_async_copy(source, weight.at[count - 1, rows], sem.at[count - 1 + at])
        )
    load = pltpu.make_async_copy(heads, held, sem.at[count + 1])
    load.start()
    for copy in copies:
        copy.start()
    load.wait()
    wide = 1024
    for at in range(count):
        copies[at].wait()
        if at == count - 1:
            copies[count].wait()
        rows = pl.ds(pl.multiple_of(order[at] * share, share), share)
        x = held[rows, :]
        for start in range(0, full, wide):
            span = slice(start, start + wide)
            term = jnp.dot(x, weight[at, :, span], preferred_element_type=F32)
            total[:, span] = term if at == 0 else total[:, span] + term
    value = total[...]
    scale = lax.rsqrt(jnp.sum(value * value, axis=1, keepdims=True) / full + EPSILON)
    for at in range(count):
        normed = total[:, at * depth : (at + 1) * depth] * scale
        out[at * share : (at + 1) * share, :] = normed.astype(BF16)


def project(order, heads, blocks, near_half, far_half):
    rows, depth = heads.shape
    count = len(blocks) + 1
    full = blocks[0].shape[1]
    share = rows // count
    return pl.pallas_call(
        functools.partial(project_kernel, full),
        out_shape=jax.ShapeDtypeStruct((rows, depth), BF16),
        in_specs=[SMEM_SPEC] + [HBM_SPEC] * (count + 2),
        out_specs=VMEM_SPEC,
        scratch_shapes=[
            pltpu.VMEM((rows, depth), BF16),
            pltpu.VMEM((count, depth, full), BF16),
            pltpu.VMEM((share, full), F32),
            pltpu.SemaphoreType.DMA((count + 2,)),
        ],
        compiler_params=params(62),
        cost_estimate=cost(2 * rows * depth * full, 9 << 20),
        name="project",
    )(order, heads, *blocks, near_half, far_half)


def ring_gather(block, size, parts):
    right = [(i, (i + 1) % size) for i in range(size)]
    left = [(i, (i - 1) % size) for i in range(size)]
    piece = block.shape[0] // parts
    pieces = [block[at * piece : (at + 1) * piece] for at in range(parts)]
    found = [pieces]
    forward, backward = list(pieces), list(pieces)
    for _ in range((size - 1) // 2):
        for at in range(parts):
            forward[at] = lax.ppermute(forward[at], "tp", right)
            backward[at] = lax.ppermute(backward[at], "tp", left)
        found += [list(forward), list(backward)]
    far = [
        lax.ppermute(forward[at], "tp", right)
        if at < parts // 2
        else lax.ppermute(backward[at], "tp", left)
        for at in range(parts)
    ]
    return found + [far]


def ring_order(size):
    me = lax.axis_index("tp")
    steps = [0]
    for step in range(1, (size - 1) // 2 + 1):
        steps += [-step, step]
    steps.append(size // 2)
    return (me + jnp.array(steps, jnp.int32) + size) % size


def weight_moves(owners, size):
    onward = []
    swap = []
    for r in range(owners):
        for t in range(size):
            to = (t + (1 if r % 2 == 0 else -1)) % size
            onward.append((r * size + t, r * size + to))
            swap.append((r * size + t, (r ^ 1) * size + t))
    return onward, swap


def after(value, *others):
    return lax.optimization_barrier((value, *others))[0]


def body(
    tokens,
    q_weight,
    k_weight,
    v_weight,
    o_weight,
    q_gain,
    k_gain,
    post_gain,
    key_pool,
    value_pool,
    cache_len,
    page_table,
):
    _, block_len, feature_part = tokens.shape
    columns = q_weight.shape[1]
    owner = lax.axis_index("req")
    owners = lax.axis_size("req")
    size = lax.axis_size("tp")
    full = columns * size
    flat = tokens.reshape(block_len, feature_part)
    pool_dev, _, _ = key_pool.shape

    valid = page_table >= 0
    source = jnp.where(valid, page_table // pool_dev, -1)
    local = jnp.where(valid, page_table % pool_dev, 0)
    chosen = jnp.sum(jnp.where(source == owner, local, 0), 1)
    half = HEAD_DIM // 2
    freqs = jnp.power(jnp.float32(ROPE_BASE), -jnp.arange(half, dtype=F32) * 2.0 / HEAD_DIM)
    freqs = jnp.concatenate([freqs, freqs])[None]
    outgoing, cosine, sine = pick_pages(
        block_len, chosen, owner[None], cache_len, freqs, key_pool, value_pool
    )
    arrived = lax.all_to_all(outgoing, "req", split_axis=0, concat_axis=0, tiled=True)

    axes = ("req", "tp")
    onward, swap = weight_moves(owners, size)

    def move(value, pairs):
        return lax.ppermute(value, axes, pairs)

    order = ring_order(size)
    blocks = ring_gather(after(flat, outgoing), size, 2)
    o_1 = move(o_weight, onward)
    o_1 = after(o_1, *(piece for block in blocks[-3:] for piece in block))
    o_2 = move(o_1, onward)
    s_1 = move(o_1, swap)
    q_proj, k_proj, new_values, stat = qkv(order, blocks, q_weight, k_weight, v_weight)
    stat = lax.psum(stat, "tp")
    o_2 = after(o_2, stat)
    o_3 = move(o_2, onward)
    s_2 = move(o_2, swap)
    attended, new_keys = attend(
        full,
        owner[None],
        cache_len,
        page_table,
        stat,
        q_gain,
        k_gain,
        q_proj,
        k_proj,
        new_values,
        cosine,
        sine,
        arrived,
    )
    core = owner % 2
    share = o_weight.shape[0] // 2
    o_4 = move(lax.dynamic_slice_in_dim(o_3, core * share, share, 0), onward)
    s_3 = move(o_3, swap)
    s_4 = move(o_4, swap)
    heads = lax.all_to_all(attended, "tp", split_axis=0, concat_axis=0, tiled=True)

    me = lax.axis_index("tp")
    turn = 1 - 2 * core
    steps = [0]
    for step in range(1, (size - 1) // 2 + 1):
        steps += [-step, step]
    steps.append(size // 2)
    weight_order = (me + turn * jnp.array(steps, jnp.int32) + size) % size
    weight_order = jnp.concatenate([weight_order, core[None].astype(jnp.int32)])
    normed = project(weight_order, heads, [o_weight, o_1, s_1, o_2, s_2, o_3, s_3], o_4, s_4)
    normed = lax.all_to_all(normed, "tp", split_axis=0, concat_axis=0, tiled=True)
    mixed = flat.astype(F32) + normed.astype(F32) * post_gain.astype(F32)
    return (mixed.astype(BF16)[None], new_keys[None], new_values[None])


def solution(mesh):
    placed = (
        P("req", None, "tp"),
        P(None, "tp"),
        P(None, "tp"),
        P(None, "tp"),
        P("tp", None),
        P("tp"),
        P("tp"),
        P("tp"),
        P("req", None, "tp"),
        P("req", None, "tp"),
        P(),
        P(),
    )

    return jax.shard_map(
        body,
        mesh=mesh,
        in_specs=placed,
        out_specs=(P("req", None, "tp"), P("req", None, "tp"), P("req", None, "tp")),
        check_vma=False,
    )
```

```python
import functools

import jax
import jax.numpy as jnp
import numpy as np
from jax import lax
from jax.experimental import pallas as pl
from jax.experimental.pallas import tpu as pltpu
from jax.sharding import PartitionSpec as P


HEAD_DIM = 128
EPSILON = 1e-06
ROPE_BASE = 500000.0
NEG = -1e30
F32 = jnp.float32
BF16 = jnp.bfloat16
VMEM_SPEC = pl.BlockSpec(memory_space=pltpu.VMEM)
SMEM_SPEC = pl.BlockSpec(memory_space=pltpu.SMEM)
HBM_SPEC = pl.BlockSpec(memory_space=pltpu.HBM)


def cost(flops, moved):
    return pl.CostEstimate(flops=flops, bytes_accessed=moved, transcendentals=0)


def params(mib):
    return pltpu.CompilerParams(vmem_limit_bytes=mib << 20)


def pick_kernel(
    chosen, place, lengths, freqs, key_pool, value_pool, out, cosine, sine, held, sem
):
    slots, page = out.shape[0], key_pool.shape[1]
    group = 8
    for slot in range(slots):
        index = chosen[slot]
        for part, pool in enumerate((key_pool, value_pool)):
            pltpu.make_async_copy(
                pool.at[index], held.at[slot, pl.ds(part * page, page)], sem.at[0, slot // group]
            ).start()

    length = lengths[place[0]]
    rows = cosine.shape[0]
    tile = 256
    for start in range(0, rows, tile):
        row = lax.broadcasted_iota(jnp.int32, (tile, 128), 0)
        lane = lax.broadcasted_iota(jnp.int32, (tile, 128), 1)
        angles = (row + (length + start)).astype(F32) * freqs[...]
        cosine[start : start + tile, :] = jnp.cos(angles)
        turned = jnp.sin(angles)
        sine[start : start + tile, :] = jnp.where(lane < 64, -turned, turned)

    leaving = []
    for at in range(0, slots, group):
        here = pl.ds(at, group)
        pltpu.make_async_copy(out.at[here], held.at[here], sem.at[0, at // group]).wait()
        leaving.append(pltpu.make_async_copy(held.at[here], out.at[here], sem.at[1, at // group]))
        leaving[-1].start()
    for copy in leaving:
        copy.wait()


def pick_pages(rows, chosen, place, lengths, freqs, key_pool, value_pool):
    slots = chosen.shape[0]
    _, page, width = key_pool.shape
    return pl.pallas_call(
        pick_kernel,
        out_shape=(
            jax.ShapeDtypeStruct((slots, 2 * page, width), BF16),
            jax.ShapeDtypeStruct((rows, HEAD_DIM), F32),
            jax.ShapeDtypeStruct((rows, HEAD_DIM), F32),
        ),
        in_specs=[SMEM_SPEC] * 3 + [VMEM_SPEC, HBM_SPEC, HBM_SPEC],
        out_specs=(HBM_SPEC, VMEM_SPEC, VMEM_SPEC),
        scratch_shapes=[
            pltpu.VMEM((slots, 2 * page, width), BF16),
            pltpu.SemaphoreType.DMA((2, slots // 8)),
        ],
        compiler_params=params(62),
        name="pick_pages",
    )(chosen, place, lengths, freqs, key_pool, value_pool)


def row_sums(values):
    squares = values * values
    folded = squares[:, :128]
    for start in range(128, values.shape[1], 128):
        folded = folded + squares[:, start : start + 128]
    return jnp.sum(folded.T, axis=0, keepdims=True)


def qkv_kernel(places, full_count, far_count, carried, last, order, *refs):
    refs = list(refs)
    blocks = [refs.pop(0) for _ in range(full_count)]
    far = [refs.pop(0) for _ in range(far_count)]
    sources = [refs.pop(0) for _ in range(3)]
    before = refs.pop(0) if carried else None
    outs = [refs.pop(0) for _ in range(3)] if last else [refs.pop(0)]
    stat = refs.pop(0) if last else None
    x, w, raw, values, sem, w_sem, out_sem = refs
    count, rows, depth = x.shape
    tile = 256
    piece = rows // 2

    def weight_copy(at, which):
        span = pl.ds(pl.multiple_of(order[places[at]] * depth, depth), depth)
        return pltpu.make_async_copy(sources[which].at[span], w.at[which, at], w_sem.at[which])

    def weight_wait(which):
        pltpu.make_async_copy(w.at[which], w.at[which], w_sem.at[which]).wait()

    def carry(which):
        return pltpu.make_async_copy(before.at[which], raw.at[which], w_sem.at[3 + which])

    def part_copy(at, part):
        here = pl.ds(part * piece, piece)
        source = blocks[at].at[here] if at < full_count else far[part]
        return pltpu.make_async_copy(source, x.at[at, here], sem.at[part])

    def part_wait(part):
        whole = x.at[:, pl.ds(part * piece, piece)]
        pltpu.make_async_copy(whole, whole, sem.at[part]).wait()

    for which in range(3):
        for at in range(count):
            weight_copy(at, which).start()
        if which == 0:
            for at in range(count):
                part_copy(at, 0).start()
        if carried:
            carry(which).start()
    for at in range(count):
        part_copy(at, 1).start()
    ready = 0
    leaving = []
    for start in range(0, rows, tile):
        here = slice(start, start + tile)
        needed = -(-(start + tile) // piece)
        for which in range(3):
            if start == 0:
                weight_wait(which)
                if carried:
                    carry(which).wait()
            for part in range(ready, needed):
                part_wait(part)
            ready = needed
            total = raw[which, here, :] if carried else None
            for at in range(count):
                term = jnp.dot(x[at, here, :], w[which, at], preferred_element_type=F32)
                total = term if total is None else total + term
            span = pl.ds(start, tile)
            if last and which == 2:
                values[here, :] = total.astype(BF16)
                held, out = values.at[span], outs[2].at[span]
            else:
                raw[which, here, :] = total
                held = raw.at[which, span]
                out = outs[which].at[span] if last else outs[0].at[which, span]
            if last and which < 2:
                stat[which : which + 1, here] = row_sums(total)
            leaving.append(pltpu.make_async_copy(held, out, out_sem.at[which, start // tile]))
            leaving[-1].start()
    for copy in leaving:
        copy.wait()


def qkv(order, places, blocks, far, weights, before=None, last=True):
    count = len(places)
    rows, depth = blocks[0].shape
    columns = weights[0].shape[1]
    wide = jax.ShapeDtypeStruct((rows, columns), F32)
    if last:
        shapes = (
            wide,
            wide,
            jax.ShapeDtypeStruct((rows, columns), BF16),
            jax.ShapeDtypeStruct((2, rows), F32),
        )
        specs = (HBM_SPEC, HBM_SPEC, HBM_SPEC, VMEM_SPEC)
    else:
        shapes = jax.ShapeDtypeStruct((3, rows, columns), F32)
        specs = HBM_SPEC
    carried = [] if before is None else [before]
    operands = [*blocks, *far, *weights, *carried]
    return pl.pallas_call(
        functools.partial(qkv_kernel, places, len(blocks), len(far), bool(carried), last),
        out_shape=shapes,
        in_specs=[SMEM_SPEC] + [HBM_SPEC] * len(operands),
        out_specs=specs,
        scratch_shapes=[
            pltpu.VMEM((count, rows, depth), BF16),
            pltpu.VMEM((3, count, depth, columns), BF16),
            pltpu.VMEM((3, rows, columns), F32),
            pltpu.VMEM((rows, columns), BF16),
            pltpu.SemaphoreType.DMA((2,)),
            pltpu.SemaphoreType.DMA((6,)),
            pltpu.SemaphoreType.DMA((3, rows // 256)),
        ],
        compiler_params=params(62),
        cost_estimate=cost(2 * rows * depth * count * 3 * columns, 9 << 20),
        name="qkv_last" if last else "qkv_early",
    )(order, *operands)


def down_rows(line):
    return jnp.broadcast_to(line, (128, line.shape[1])).T


def attend_kernel(
    full,
    place,
    lengths,
    page_table,
    stat,
    q_gain,
    k_gain,
    q_hbm,
    k_hbm,
    v_hbm,
    cos_hbm,
    sin_hbm,
    pages_hbm,
    out,
    keys_out,
    raw,
    table,
    query,
    new_k,
    new_v,
    pages,
    ones,
    scores,
    result_rows,
    counts,
    sem,
    page_sem,
    out_sem,
):
    tile = 256
    slots = pages.shape[0]
    rows, columns = query.shape
    page = pages.shape[1] // 2
    group = 8
    span = group * page
    cached = slots * page
    factor = HEAD_DIM**-0.5 * 1.4426950408889634
    contract = (((1,), (1,)), ((), ()))
    small = [
        pltpu.make_async_copy(source, held, sem.at[at])
        for at, (source, held) in enumerate(
            (
                (q_hbm, raw.at[0]),
                (cos_hbm, table.at[0]),
                (sin_hbm, table.at[1]),
                (k_hbm, raw.at[1]),
                (v_hbm, new_v),
            )
        )
    ]
    for copy in small:
        copy.start()
    parts = [
        pltpu.make_async_copy(
            pages_hbm.at[pl.ds(at, group)], pages.at[pl.ds(at, group)], page_sem.at[at // group]
        )
        for at in range(0, slots, group)
    ]
    for copy in parts:
        copy.start()

    owner = place[0]
    length = lengths[owner]
    ones[...] = jnp.ones(ones.shape, BF16)

    @pl.loop(0, slots)
    def _(slot):
        counts[slot] = 0

    @pl.loop(0, page_table.shape[1])
    def _(at):
        entry = page_table[owner, at]

        @pl.when(entry >= 0)
        def _():
            counts[lax.div(entry, slots)] = length - at * page

    for which, gain in enumerate((q_gain, k_gain)):
        for copy in small[:3] if which == 0 else small[3:4]:
            copy.wait()
        for start in range(0, rows, tile):
            here = slice(start, start + tile)
            scale = lax.rsqrt(down_rows(stat[which : which + 1, here]) / full + EPSILON)
            for low in range(0, columns, HEAD_DIM):
                lanes = slice(low, low + HEAD_DIM)
                value = raw[which, here, lanes] * scale * gain[lanes].astype(F32)[None]
                turned = value * table[0, here, :]
                turned = turned + pltpu.roll(value, HEAD_DIM // 2, 1) * table[1, here, :]
                turned = turned.astype(BF16)
                if which == 0:
                    query[here, lanes] = turned
                else:
                    new_k[here, lanes] = turned
    leaving = [pltpu.make_async_copy(new_k, keys_out, out_sem.at[0])]
    leaving[0].start()
    small[4].wait()
    for copy in parts:
        copy.wait()

    first = lax.div(page_table[owner, 0], slots)
    key = jnp.broadcast_to(pages[first, 0:1, :], (page, columns))

    @pl.loop(0, slots)
    def _(slot):
        exist = counts[slot]

        @pl.when(exist < page)
        def _():
            for low in range(0, columns, 128):
                lanes = slice(low, low + 128)
                row = lax.broadcasted_iota(jnp.int32, (page, 128), 0)
                keep = row < exist
                kept = pages[slot, :page, lanes].astype(F32)
                spare = key[:, lanes].astype(F32)
                pages[slot, :page, lanes] = jnp.where(keep, kept, spare).astype(BF16)
                value = pages[slot, page:, lanes].astype(F32)
                pages[slot, page:, lanes] = jnp.where(keep, value, 0.0).astype(BF16)
                if low == 0:
                    ones[slot] = jnp.where(keep, 1.0, 0.0).astype(BF16)

    one = jnp.ones((tile, HEAD_DIM), BF16)
    for column in range(0, columns, HEAD_DIM):
        head = slice(column, column + HEAD_DIM)
        for start in range(0, rows, tile):
            q = query[start : start + tile, head]
            fresh = start + tile
            top = None
            for at in range(0, slots, group):
                k = pages[at : at + group, :page, head].reshape(span, HEAD_DIM)
                s = lax.dot_general(q, k, contract, preferred_element_type=F32)
                scores[:, at * page : at * page + span] = s
                for lane in range(0, span, 128):
                    part = s[:, lane : lane + 128]
                    top = part if top is None else jnp.maximum(top, part)
            for low in range(0, fresh, tile):
                k = new_k[low : low + tile, head]
                s = lax.dot_general(q, k, contract, preferred_element_type=F32)
                if low == start:
                    row = lax.broadcasted_iota(jnp.int32, s.shape, 0)
                    col = lax.broadcasted_iota(jnp.int32, s.shape, 1)
                    s = jnp.where(row >= col, s, NEG)
                scores[:, cached + low : cached + low + tile] = s
                for lane in range(0, tile, 128):
                    top = jnp.maximum(top, s[:, lane : lane + 128])
            peak = jnp.max(top, axis=1, keepdims=True)
            result = None
            for at in range(0, slots, group):
                raised = jnp.exp2((scores[:, at * page : at * page + span] - peak) * factor)
                v = jnp.concatenate(
                    [
                        pages[at : at + group, page:, head].reshape(span, HEAD_DIM),
                        ones[at : at + group].reshape(span, HEAD_DIM),
                    ],
                    1,
                )
                term = jnp.dot(raised.astype(BF16), v, preferred_element_type=F32)
                result = term if result is None else result + term
            for low in range(0, fresh, tile):
                raised = jnp.exp2(
                    (scores[:, cached + low : cached + low + tile] - peak) * factor
                )
                v = jnp.concatenate([new_v[low : low + tile, head], one], 1)
                result = result + jnp.dot(raised.astype(BF16), v, preferred_element_type=F32)
            result = result[:, :HEAD_DIM] / result[:, HEAD_DIM:]
            result_rows[start : start + tile, head] = result.astype(BF16)
            if column + HEAD_DIM == columns:
                here = pl.ds(start, tile)
                leaving.append(
                    pltpu.make_async_copy(
                        result_rows.at[here], out.at[here], out_sem.at[1 + start // tile]
                    )
                )
                leaving[-1].start()
    for copy in leaving:
        copy.wait()


def attend(
    full, place, lengths, page_table, stat, q_gain, k_gain, q_proj, k_proj, new_v, cosine, sine, pages
):
    rows, columns = q_proj.shape
    slots, both, _ = pages.shape
    keys = slots * both // 2 + rows
    held = pltpu.VMEM((rows, columns), BF16)
    shape = jax.ShapeDtypeStruct((rows, columns), BF16)
    return pl.pallas_call(
        functools.partial(attend_kernel, full),
        out_shape=(shape, shape),
        in_specs=[SMEM_SPEC] * 3 + [VMEM_SPEC] * 3 + [HBM_SPEC] * 6,
        out_specs=(HBM_SPEC, HBM_SPEC),
        scratch_shapes=[
            pltpu.VMEM((2, rows, columns), F32),
            pltpu.VMEM((2, rows, HEAD_DIM), F32),
            held,
            held,
            held,
            pltpu.VMEM((slots, both, columns), BF16),
            pltpu.VMEM((slots, both // 2, HEAD_DIM), BF16),
            pltpu.VMEM((256, keys), F32),
            held,
            pltpu.SMEM((slots,), jnp.int32),
            pltpu.SemaphoreType.DMA((5,)),
            pltpu.SemaphoreType.DMA((slots,)),
            pltpu.SemaphoreType.DMA((1 + rows // 256,)),
        ],
        compiler_params=params(62),
        cost_estimate=cost(4 * rows * keys * columns, 9 << 20),
        name="attend",
    )(place, lengths, page_table, stat, q_gain, k_gain, q_proj, k_proj, new_v, cosine, sine, pages)


def project_kernel(full, order, *refs):
    heads, *blocks, near_half, far_half, out, held, weight, total, sem = refs
    count = len(blocks) + 1
    depth = heads.shape[1]
    share = total.shape[0]
    half = depth // 2
    core = order[count]
    copies = [
        pltpu.make_async_copy(block, weight.at[at], sem.at[at]) for at, block in enumerate(blocks)
    ]
    for at, (source, offset) in enumerate(((near_half, core), (far_half, 1 - core))):
        rows = pl.ds(pl.multiple_of(offset * half, half), half)
        copies.append(
            pltpu.make_async_copy(source, weight.at[count - 1, rows], sem.at[count - 1 + at])
        )
    load = pltpu.make_async_copy(heads, held, sem.at[count + 1])
    load.start()
    for copy in copies:
        copy.start()
    load.wait()
    wide = 1024
    for at in range(count):
        copies[at].wait()
        if at == count - 1:
            copies[count].wait()
        rows = pl.ds(pl.multiple_of(order[at] * share, share), share)
        x = held[rows, :]
        for start in range(0, full, wide):
            span = slice(start, start + wide)
            term = jnp.dot(x, weight[at, :, span], preferred_element_type=F32)
            total[:, span] = term if at == 0 else total[:, span] + term
    value = total[...]
    scale = lax.rsqrt(jnp.sum(value * value, axis=1, keepdims=True) / full + EPSILON)
    for at in range(count):
        normed = total[:, at * depth : (at + 1) * depth] * scale
        out[at * share : (at + 1) * share, :] = normed.astype(BF16)


def project(order, heads, blocks, near_half, far_half):
    rows, depth = heads.shape
    count = len(blocks) + 1
    full = blocks[0].shape[1]
    share = rows // count
    return pl.pallas_call(
        functools.partial(project_kernel, full),
        out_shape=jax.ShapeDtypeStruct((rows, depth), BF16),
        in_specs=[SMEM_SPEC] + [HBM_SPEC] * (count + 2),
        out_specs=VMEM_SPEC,
        scratch_shapes=[
            pltpu.VMEM((rows, depth), BF16),
            pltpu.VMEM((count, depth, full), BF16),
            pltpu.VMEM((share, full), F32),
            pltpu.SemaphoreType.DMA((count + 2,)),
        ],
        compiler_params=params(62),
        cost_estimate=cost(2 * rows * depth * full, 9 << 20),
        name="project",
    )(order, heads, *blocks, near_half, far_half)


def ring_gather(block, size):
    right = [(i, (i + 1) % size) for i in range(size)]
    left = [(i, (i - 1) % size) for i in range(size)]
    found = [block]
    forward = backward = block
    for _ in range((size - 1) // 2):
        forward = lax.ppermute(forward, "tp", right)
        backward = lax.ppermute(backward, "tp", left)
        found += [forward, backward]
    half = block.shape[0] // 2
    far = [
        lax.ppermute(forward[:half], "tp", right),
        lax.ppermute(backward[half:], "tp", left),
    ]
    return found, far


def ring_order(size):
    me = lax.axis_index("tp")
    steps = [0]
    for step in range(1, (size - 1) // 2 + 1):
        steps += [-step, step]
    steps.append(size // 2)
    return (me + jnp.array(steps, jnp.int32) + size) % size


def weight_moves(owners, size):
    onward = []
    swap = []
    for r in range(owners):
        for t in range(size):
            to = (t + (1 if r % 2 == 0 else -1)) % size
            onward.append((r * size + t, r * size + to))
            swap.append((r * size + t, (r ^ 1) * size + t))
    return onward, swap


def after(value, *others):
    return lax.optimization_barrier((value, *others))[0]


def body(
    tokens,
    q_weight,
    k_weight,
    v_weight,
    o_weight,
    q_gain,
    k_gain,
    post_gain,
    key_pool,
    value_pool,
    cache_len,
    page_table,
):
    _, block_len, feature_part = tokens.shape
    columns = q_weight.shape[1]
    owner = lax.axis_index("req")
    owners = lax.axis_size("req")
    size = lax.axis_size("tp")
    full = columns * size
    flat = tokens.reshape(block_len, feature_part)
    pool_dev, _, _ = key_pool.shape

    valid = page_table >= 0
    source = jnp.where(valid, page_table // pool_dev, -1)
    local = jnp.where(valid, page_table % pool_dev, 0)
    chosen = jnp.sum(jnp.where(source == owner, local, 0), 1)
    half = HEAD_DIM // 2
    freqs = np.power(np.float32(ROPE_BASE), -np.arange(half, dtype=np.float32) * 2.0 / HEAD_DIM)
    freqs = jnp.asarray(np.concatenate([freqs, freqs])[None].astype(np.float32))
    outgoing, cosine, sine = pick_pages(
        block_len, chosen, owner[None], cache_len, freqs, key_pool, value_pool
    )
    arrived = lax.all_to_all(outgoing, "req", split_axis=0, concat_axis=0, tiled=True)

    axes = ("req", "tp")
    onward, swap = weight_moves(owners, size)

    def move(value, pairs):
        return lax.ppermute(value, axes, pairs)

    order = ring_order(size)
    blocks, far = ring_gather(after(flat, outgoing), size)
    o_1 = move(o_weight, onward)
    weights = (q_weight, k_weight, v_weight)
    known = size - 3
    sums = qkv(order, tuple(range(known)), blocks[:known], [], weights, last=False)
    o_1 = after(o_1, blocks[-1], blocks[-2])
    o_2 = move(o_1, onward)
    s_1 = move(o_1, swap)
    q_proj, k_proj, new_values, stat = qkv(
        order, tuple(range(known, size)), blocks[known:], far, weights, before=sums
    )
    stat = lax.psum(stat, "tp")
    o_2 = after(o_2, stat)
    o_3 = move(o_2, onward)
    s_2 = move(o_2, swap)
    attended, new_keys = attend(
        full,
        owner[None],
        cache_len,
        page_table,
        stat,
        q_gain,
        k_gain,
        q_proj,
        k_proj,
        new_values,
        cosine,
        sine,
        arrived,
    )
    core = owner % 2
    share = o_weight.shape[0] // 2
    o_4 = move(lax.dynamic_slice_in_dim(o_3, core * share, share, 0), onward)
    s_3 = move(o_3, swap)
    s_4 = move(o_4, swap)
    heads = lax.all_to_all(attended, "tp", split_axis=0, concat_axis=0, tiled=True)

    me = after(lax.axis_index("tp"), s_1, s_2, s_3, s_4)
    turn = 1 - 2 * core
    steps = [0]
    for step in range(1, (size - 1) // 2 + 1):
        steps += [-step, step]
    steps.append(size // 2)
    weight_order = (me + turn * jnp.array(steps, jnp.int32) + size) % size
    weight_order = jnp.concatenate([weight_order, core[None].astype(jnp.int32)])
    normed = project(weight_order, heads, [o_weight, o_1, s_1, o_2, s_2, o_3, s_3], o_4, s_4)
    normed = lax.all_to_all(normed, "tp", split_axis=0, concat_axis=0, tiled=True)
    mixed = flat.astype(F32) + normed.astype(F32) * post_gain.astype(F32)
    return (mixed.astype(BF16)[None], new_keys[None], new_values[None])


def solution(mesh):
    placed = (
        P("req", None, "tp"),
        P(None, "tp"),
        P(None, "tp"),
        P(None, "tp"),
        P("tp", None),
        P("tp"),
        P("tp"),
        P("tp"),
        P("req", None, "tp"),
        P("req", None, "tp"),
        P(),
        P(),
    )

    return jax.shard_map(
        body,
        mesh=mesh,
        in_specs=placed,
        out_specs=(P("req", None, "tp"), P("req", None, "tp"), P("req", None, "tp")),
        check_vma=False,
    )
```

```python
import functools

import jax
import jax.numpy as jnp
import numpy as np
from jax import lax
from jax.experimental import pallas as pl
from jax.experimental.pallas import tpu as pltpu
from jax.sharding import PartitionSpec as P


HEAD_DIM = 128
EPSILON = 1e-06
ROPE_BASE = 500000.0
NEG = -1e30
F32 = jnp.float32
BF16 = jnp.bfloat16
VMEM_SPEC = pl.BlockSpec(memory_space=pltpu.VMEM)
SMEM_SPEC = pl.BlockSpec(memory_space=pltpu.SMEM)
HBM_SPEC = pl.BlockSpec(memory_space=pltpu.HBM)


def cost(flops, moved):
    return pl.CostEstimate(flops=flops, bytes_accessed=moved, transcendentals=0)


def params(mib):
    return pltpu.CompilerParams(vmem_limit_bytes=mib << 20)


def pick_kernel(
    chosen, place, lengths, freqs, key_pool, value_pool, out, cosine, sine, held, sem
):
    slots, page = out.shape[0], key_pool.shape[1]
    group = 8
    for slot in range(slots):
        index = chosen[slot]
        for part, pool in enumerate((key_pool, value_pool)):
            pltpu.make_async_copy(
                pool.at[index], held.at[slot, pl.ds(part * page, page)], sem.at[0, slot // group]
            ).start()

    length = lengths[place[0]]
    rows = cosine.shape[0]
    tile = 256
    for start in range(0, rows, tile):
        row = lax.broadcasted_iota(jnp.int32, (tile, 128), 0)
        lane = lax.broadcasted_iota(jnp.int32, (tile, 128), 1)
        angles = (row + (length + start)).astype(F32) * freqs[...]
        cosine[start : start + tile, :] = jnp.cos(angles)
        turned = jnp.sin(angles)
        sine[start : start + tile, :] = jnp.where(lane < 64, -turned, turned)

    leaving = []
    for at in range(0, slots, group):
        here = pl.ds(at, group)
        pltpu.make_async_copy(out.at[here], held.at[here], sem.at[0, at // group]).wait()
        leaving.append(pltpu.make_async_copy(held.at[here], out.at[here], sem.at[1, at // group]))
        leaving[-1].start()
    for copy in leaving:
        copy.wait()


def pick_pages(rows, chosen, place, lengths, freqs, key_pool, value_pool):
    slots = chosen.shape[0]
    _, page, width = key_pool.shape
    return pl.pallas_call(
        pick_kernel,
        out_shape=(
            jax.ShapeDtypeStruct((slots, 2 * page, width), BF16),
            jax.ShapeDtypeStruct((rows, HEAD_DIM), F32),
            jax.ShapeDtypeStruct((rows, HEAD_DIM), F32),
        ),
        in_specs=[SMEM_SPEC] * 3 + [VMEM_SPEC, HBM_SPEC, HBM_SPEC],
        out_specs=(HBM_SPEC, VMEM_SPEC, VMEM_SPEC),
        scratch_shapes=[
            pltpu.VMEM((slots, 2 * page, width), BF16),
            pltpu.SemaphoreType.DMA((2, slots // 8)),
        ],
        compiler_params=params(62),
        name="pick_pages",
    )(chosen, place, lengths, freqs, key_pool, value_pool)


def row_sums(values):
    squares = values * values
    folded = squares[:, :128]
    for start in range(128, values.shape[1], 128):
        folded = folded + squares[:, start : start + 128]
    return jnp.sum(folded.T, axis=0, keepdims=True)


def qkv_kernel(count, parts, order, *refs):
    blocks = refs[: count * parts]
    wq, wk, wv, q_out, k_out, v_out, stat, x, w, raw, values, sem, w_sem, out_sem = refs[
        count * parts :
    ]
    depth = x.shape[2]
    rows = x.shape[1]
    piece = rows // parts

    def weight_copy(which, source):
        return pltpu.make_async_copy(source, w.at[which], w_sem.at[which])

    def part_copy(at, part):
        return pltpu.make_async_copy(
            blocks[at * parts + part], x.at[at, pl.ds(part * piece, piece)], sem.at[part]
        )

    def part_wait(part):
        whole = x.at[:, pl.ds(part * piece, piece)]
        pltpu.make_async_copy(whole, whole, sem.at[part]).wait()

    weight_copy(0, wq).start()
    for at in range(count):
        part_copy(at, 0).start()
    weight_copy(1, wk).start()
    weight_copy(2, wv).start()
    for part in range(1, parts):
        for at in range(count):
            part_copy(at, part).start()
    tile = 256
    ready = 0
    leaving = []
    for start in range(0, rows, tile):
        here = slice(start, start + tile)
        needed = -(-(start + tile) // piece)
        for which, source in enumerate((wq, wk, wv)):
            if start == 0:
                weight_copy(which, source).wait()
            for part in range(ready, needed):
                part_wait(part)
            ready = needed
            total = None
            for at in range(count):
                span = pl.ds(pl.multiple_of(order[at] * depth, depth), depth)
                term = jnp.dot(x[at, here, :], w[which, span, :], preferred_element_type=F32)
                total = term if total is None else total + term
            if which < 2:
                raw[which, here, :] = total
                stat[which : which + 1, here] = row_sums(total)
                held, out = raw.at[which], (q_out, k_out)[which]
            else:
                values[here, :] = total.astype(BF16)
                held, out = values, v_out
            span = pl.ds(start, tile)
            leaving.append(
                pltpu.make_async_copy(
                    held.at[span], out.at[span], out_sem.at[which, start // tile]
                )
            )
            leaving[-1].start()
    for copy in leaving:
        copy.wait()


def qkv(order, blocks, wq, wk, wv):
    count = len(blocks)
    parts = len(blocks[0])
    piece, depth = blocks[0][0].shape
    rows = piece * parts
    columns = wq.shape[1]
    return pl.pallas_call(
        functools.partial(qkv_kernel, count, parts),
        out_shape=(
            jax.ShapeDtypeStruct((rows, columns), F32),
            jax.ShapeDtypeStruct((rows, columns), F32),
            jax.ShapeDtypeStruct((rows, columns), BF16),
            jax.ShapeDtypeStruct((2, rows), F32),
        ),
        in_specs=[SMEM_SPEC] + [HBM_SPEC] * (count * parts + 3),
        out_specs=(HBM_SPEC, HBM_SPEC, HBM_SPEC, VMEM_SPEC),
        scratch_shapes=[
            pltpu.VMEM((count, rows, depth), BF16),
            pltpu.VMEM((3, wq.shape[0], columns), BF16),
            pltpu.VMEM((2, rows, columns), F32),
            pltpu.VMEM((rows, columns), BF16),
            pltpu.SemaphoreType.DMA((parts,)),
            pltpu.SemaphoreType.DMA((3,)),
            pltpu.SemaphoreType.DMA((3, rows // 256)),
        ],
        compiler_params=params(62),
        cost_estimate=cost(2 * rows * depth * count * 3 * columns, 9 << 20),
        name="qkv",
    )(order, *[piece for block in blocks for piece in block], wq, wk, wv)


def down_rows(line):
    return jnp.broadcast_to(line, (128, line.shape[1])).T


def attend_kernel(
    full,
    place,
    lengths,
    page_table,
    stat,
    q_gain,
    k_gain,
    q_hbm,
    k_hbm,
    v_hbm,
    cos_hbm,
    sin_hbm,
    pages_hbm,
    out,
    keys_out,
    raw,
    table,
    query,
    new_k,
    new_v,
    pages,
    ones,
    scores,
    result_rows,
    counts,
    sem,
    page_sem,
    out_sem,
):
    tile = 256
    slots = pages.shape[0]
    rows, columns = query.shape
    page = pages.shape[1] // 2
    group = 8
    span = group * page
    cached = slots * page
    factor = HEAD_DIM**-0.5 * 1.4426950408889634
    contract = (((1,), (1,)), ((), ()))
    small = [
        pltpu.make_async_copy(source, held, sem.at[at])
        for at, (source, held) in enumerate(
            (
                (q_hbm, raw.at[0]),
                (cos_hbm, table.at[0]),
                (sin_hbm, table.at[1]),
                (k_hbm, raw.at[1]),
                (v_hbm, new_v),
            )
        )
    ]
    for copy in small:
        copy.start()
    parts = [
        pltpu.make_async_copy(
            pages_hbm.at[pl.ds(at, group)], pages.at[pl.ds(at, group)], page_sem.at[at // group]
        )
        for at in range(0, slots, group)
    ]
    for copy in parts:
        copy.start()

    owner = place[0]
    length = lengths[owner]
    ones[...] = jnp.ones(ones.shape, BF16)

    @pl.loop(0, slots)
    def _(slot):
        counts[slot] = 0

    @pl.loop(0, page_table.shape[1])
    def _(at):
        entry = page_table[owner, at]

        @pl.when(entry >= 0)
        def _():
            counts[lax.div(entry, slots)] = length - at * page

    for which, gain in enumerate((q_gain, k_gain)):
        for copy in small[:3] if which == 0 else small[3:4]:
            copy.wait()
        for start in range(0, rows, tile):
            here = slice(start, start + tile)
            scale = lax.rsqrt(down_rows(stat[which : which + 1, here]) / full + EPSILON)
            for low in range(0, columns, HEAD_DIM):
                lanes = slice(low, low + HEAD_DIM)
                value = raw[which, here, lanes] * scale * gain[lanes].astype(F32)[None]
                turned = value * table[0, here, :]
                turned = turned + pltpu.roll(value, HEAD_DIM // 2, 1) * table[1, here, :]
                turned = turned.astype(BF16)
                if which == 0:
                    query[here, lanes] = turned
                else:
                    new_k[here, lanes] = turned
    leaving = [pltpu.make_async_copy(new_k, keys_out, out_sem.at[0])]
    leaving[0].start()
    small[4].wait()
    for copy in parts:
        copy.wait()

    first = lax.div(page_table[owner, 0], slots)
    key = jnp.broadcast_to(pages[first, 0:1, :], (page, columns))

    @pl.loop(0, slots)
    def _(slot):
        exist = counts[slot]

        @pl.when(exist < page)
        def _():
            for low in range(0, columns, 128):
                lanes = slice(low, low + 128)
                row = lax.broadcasted_iota(jnp.int32, (page, 128), 0)
                keep = row < exist
                kept = pages[slot, :page, lanes].astype(F32)
                spare = key[:, lanes].astype(F32)
                pages[slot, :page, lanes] = jnp.where(keep, kept, spare).astype(BF16)
                value = pages[slot, page:, lanes].astype(F32)
                pages[slot, page:, lanes] = jnp.where(keep, value, 0.0).astype(BF16)
                if low == 0:
                    ones[slot] = jnp.where(keep, 1.0, 0.0).astype(BF16)

    one = jnp.ones((tile, HEAD_DIM), BF16)
    for column in range(0, columns, HEAD_DIM):
        head = slice(column, column + HEAD_DIM)
        for start in range(0, rows, tile):
            q = query[start : start + tile, head]
            fresh = start + tile
            top = None
            for at in range(0, slots, group):
                k = pages[at : at + group, :page, head].reshape(span, HEAD_DIM)
                s = lax.dot_general(q, k, contract, preferred_element_type=F32)
                scores[:, at * page : at * page + span] = s
                for lane in range(0, span, 128):
                    part = s[:, lane : lane + 128]
                    top = part if top is None else jnp.maximum(top, part)
            for low in range(0, fresh, tile):
                k = new_k[low : low + tile, head]
                s = lax.dot_general(q, k, contract, preferred_element_type=F32)
                if low == start:
                    row = lax.broadcasted_iota(jnp.int32, s.shape, 0)
                    col = lax.broadcasted_iota(jnp.int32, s.shape, 1)
                    s = jnp.where(row >= col, s, NEG)
                scores[:, cached + low : cached + low + tile] = s
                for lane in range(0, tile, 128):
                    top = jnp.maximum(top, s[:, lane : lane + 128])
            peak = jnp.max(top, axis=1, keepdims=True)
            result = None
            for at in range(0, slots, group):
                raised = jnp.exp2((scores[:, at * page : at * page + span] - peak) * factor)
                v = jnp.concatenate(
                    [
                        pages[at : at + group, page:, head].reshape(span, HEAD_DIM),
                        ones[at : at + group].reshape(span, HEAD_DIM),
                    ],
                    1,
                )
                term = jnp.dot(raised.astype(BF16), v, preferred_element_type=F32)
                result = term if result is None else result + term
            for low in range(0, fresh, tile):
                raised = jnp.exp2(
                    (scores[:, cached + low : cached + low + tile] - peak) * factor
                )
                v = jnp.concatenate([new_v[low : low + tile, head], one], 1)
                result = result + jnp.dot(raised.astype(BF16), v, preferred_element_type=F32)
            result = result[:, :HEAD_DIM] / result[:, HEAD_DIM:]
            result_rows[start : start + tile, head] = result.astype(BF16)
            if column + HEAD_DIM == columns:
                here = pl.ds(start, tile)
                leaving.append(
                    pltpu.make_async_copy(
                        result_rows.at[here], out.at[here], out_sem.at[1 + start // tile]
                    )
                )
                leaving[-1].start()
    for copy in leaving:
        copy.wait()


def attend(
    full, place, lengths, page_table, stat, q_gain, k_gain, q_proj, k_proj, new_v, cosine, sine, pages
):
    rows, columns = q_proj.shape
    slots, both, _ = pages.shape
    keys = slots * both // 2 + rows
    held = pltpu.VMEM((rows, columns), BF16)
    shape = jax.ShapeDtypeStruct((rows, columns), BF16)
    return pl.pallas_call(
        functools.partial(attend_kernel, full),
        out_shape=(shape, shape),
        in_specs=[SMEM_SPEC] * 3 + [VMEM_SPEC] * 3 + [HBM_SPEC] * 6,
        out_specs=(HBM_SPEC, HBM_SPEC),
        scratch_shapes=[
            pltpu.VMEM((2, rows, columns), F32),
            pltpu.VMEM((2, rows, HEAD_DIM), F32),
            held,
            held,
            held,
            pltpu.VMEM((slots, both, columns), BF16),
            pltpu.VMEM((slots, both // 2, HEAD_DIM), BF16),
            pltpu.VMEM((256, keys), F32),
            held,
            pltpu.SMEM((slots,), jnp.int32),
            pltpu.SemaphoreType.DMA((5,)),
            pltpu.SemaphoreType.DMA((slots,)),
            pltpu.SemaphoreType.DMA((1 + rows // 256,)),
        ],
        compiler_params=params(62),
        cost_estimate=cost(4 * rows * keys * columns, 9 << 20),
        name="attend",
    )(place, lengths, page_table, stat, q_gain, k_gain, q_proj, k_proj, new_v, cosine, sine, pages)


def project_kernel(full, order, *refs):
    heads, *blocks, near_half, far_half, out, held, weight, total, sem = refs
    count = len(blocks) + 1
    depth = heads.shape[1]
    share = total.shape[0]
    half = depth // 2
    core = order[count]
    copies = [
        pltpu.make_async_copy(block, weight.at[at], sem.at[at]) for at, block in enumerate(blocks)
    ]
    for at, (source, offset) in enumerate(((near_half, core), (far_half, 1 - core))):
        rows = pl.ds(pl.multiple_of(offset * half, half), half)
        copies.append(
            pltpu.make_async_copy(source, weight.at[count - 1, rows], sem.at[count - 1 + at])
        )
    load = pltpu.make_async_copy(heads, held, sem.at[count + 1])
    load.start()
    for copy in copies:
        copy.start()
    load.wait()
    wide = 1024
    for at in range(count):
        copies[at].wait()
        if at == count - 1:
            copies[count].wait()
        rows = pl.ds(pl.multiple_of(order[at] * share, share), share)
        x = held[rows, :]
        for start in range(0, full, wide):
            span = slice(start, start + wide)
            term = jnp.dot(x, weight[at, :, span], preferred_element_type=F32)
            total[:, span] = term if at == 0 else total[:, span] + term
    value = total[...]
    scale = lax.rsqrt(jnp.sum(value * value, axis=1, keepdims=True) / full + EPSILON)
    for at in range(count):
        normed = total[:, at * depth : (at + 1) * depth] * scale
        out[at * share : (at + 1) * share, :] = normed.astype(BF16)


def project(order, heads, blocks, near_half, far_half):
    rows, depth = heads.shape
    count = len(blocks) + 1
    full = blocks[0].shape[1]
    share = rows // count
    return pl.pallas_call(
        functools.partial(project_kernel, full),
        out_shape=jax.ShapeDtypeStruct((rows, depth), BF16),
        in_specs=[SMEM_SPEC] + [HBM_SPEC] * (count + 2),
        out_specs=VMEM_SPEC,
        scratch_shapes=[
            pltpu.VMEM((rows, depth), BF16),
            pltpu.VMEM((count, depth, full), BF16),
            pltpu.VMEM((share, full), F32),
            pltpu.SemaphoreType.DMA((count + 2,)),
        ],
        compiler_params=params(62),
        cost_estimate=cost(2 * rows * depth * full, 9 << 20),
        name="project",
    )(order, heads, *blocks, near_half, far_half)


def ring_gather(block, size, parts):
    right = [(i, (i + 1) % size) for i in range(size)]
    left = [(i, (i - 1) % size) for i in range(size)]
    piece = block.shape[0] // parts
    pieces = [block[at * piece : (at + 1) * piece] for at in range(parts)]
    found = [pieces]
    forward, backward = list(pieces), list(pieces)
    for _ in range((size - 1) // 2):
        for at in range(parts):
            forward[at] = lax.ppermute(forward[at], "tp", right)
            backward[at] = lax.ppermute(backward[at], "tp", left)
        found += [list(forward), list(backward)]
    far = [
        lax.ppermute(forward[at], "tp", right)
        if at < parts // 2
        else lax.ppermute(backward[at], "tp", left)
        for at in range(parts)
    ]
    return found + [far]


def ring_order(size):
    me = lax.axis_index("tp")
    steps = [0]
    for step in range(1, (size - 1) // 2 + 1):
        steps += [-step, step]
    steps.append(size // 2)
    return (me + jnp.array(steps, jnp.int32) + size) % size


def weight_moves(owners, size):
    onward = []
    swap = []
    for r in range(owners):
        for t in range(size):
            to = (t + (1 if r % 2 == 0 else -1)) % size
            onward.append((r * size + t, r * size + to))
            swap.append((r * size + t, (r ^ 1) * size + t))
    return onward, swap


def after(value, *others):
    return lax.optimization_barrier((value, *others))[0]


def body(
    tokens,
    q_weight,
    k_weight,
    v_weight,
    o_weight,
    q_gain,
    k_gain,
    post_gain,
    key_pool,
    value_pool,
    cache_len,
    page_table,
):
    _, block_len, feature_part = tokens.shape
    columns = q_weight.shape[1]
    owner = lax.axis_index("req")
    owners = lax.axis_size("req")
    size = lax.axis_size("tp")
    full = columns * size
    flat = tokens.reshape(block_len, feature_part)
    pool_dev, _, _ = key_pool.shape

    valid = page_table >= 0
    source = jnp.where(valid, page_table // pool_dev, -1)
    local = jnp.where(valid, page_table % pool_dev, 0)
    chosen = jnp.sum(jnp.where(source == owner, local, 0), 1)
    half = HEAD_DIM // 2
    freqs = np.power(np.float32(ROPE_BASE), -np.arange(half, dtype=np.float32) * 2.0 / HEAD_DIM)
    freqs = jnp.asarray(np.concatenate([freqs, freqs])[None].astype(np.float32))
    outgoing, cosine, sine = pick_pages(
        block_len, chosen, owner[None], cache_len, freqs, key_pool, value_pool
    )
    arrived = lax.all_to_all(outgoing, "req", split_axis=0, concat_axis=0, tiled=True)

    axes = ("req", "tp")
    onward, swap = weight_moves(owners, size)

    def move(value, pairs):
        return lax.ppermute(value, axes, pairs)

    order = ring_order(size)
    blocks = ring_gather(after(flat, outgoing), size, 2)
    o_1 = move(o_weight, onward)
    o_1 = after(o_1, *(piece for block in blocks[-3:] for piece in block))
    o_2 = move(o_1, onward)
    s_1 = move(o_1, swap)
    q_proj, k_proj, new_values, stat = qkv(order, blocks, q_weight, k_weight, v_weight)
    stat = lax.psum(stat, "tp")
    o_2 = after(o_2, stat)
    o_3 = move(o_2, onward)
    s_2 = move(o_2, swap)
    attended, new_keys = attend(
        full,
        owner[None],
        cache_len,
        page_table,
        stat,
        q_gain,
        k_gain,
        q_proj,
        k_proj,
        new_values,
        cosine,
        sine,
        arrived,
    )
    core = owner % 2
    share = o_weight.shape[0] // 2
    o_4 = move(lax.dynamic_slice_in_dim(o_3, core * share, share, 0), onward)
    s_3 = move(o_3, swap)
    s_4 = move(o_4, swap)
    heads = lax.all_to_all(attended, "tp", split_axis=0, concat_axis=0, tiled=True)

    me = after(lax.axis_index("tp"), s_1, s_2, s_3, s_4)
    turn = 1 - 2 * core
    steps = [0]
    for step in range(1, (size - 1) // 2 + 1):
        steps += [-step, step]
    steps.append(size // 2)
    weight_order = (me + turn * jnp.array(steps, jnp.int32) + size) % size
    weight_order = jnp.concatenate([weight_order, core[None].astype(jnp.int32)])
    normed = project(weight_order, heads, [o_weight, o_1, s_1, o_2, s_2, o_3, s_3], o_4, s_4)
    normed = lax.all_to_all(normed, "tp", split_axis=0, concat_axis=0, tiled=True)
    mixed = flat.astype(F32) + normed.astype(F32) * post_gain.astype(F32)
    return (mixed.astype(BF16)[None], new_keys[None], new_values[None])


def solution(mesh):
    placed = (
        P("req", None, "tp"),
        P(None, "tp"),
        P(None, "tp"),
        P(None, "tp"),
        P("tp", None),
        P("tp"),
        P("tp"),
        P("tp"),
        P("req", None, "tp"),
        P("req", None, "tp"),
        P(),
        P(),
    )

    return jax.shard_map(
        body,
        mesh=mesh,
        in_specs=placed,
        out_specs=(P("req", None, "tp"), P("req", None, "tp"), P("req", None, "tp")),
        check_vma=False,
    )
```
